32 devices in a mesh: fsdp: 8 (over y, x, core), tp: 4 (over z).
Axes of the slice: x: 2, y: 2, z: 4, core: 2. Of those that a mesh axis runs over, the one named last changes fastest.
Arguments:
- layer_input: bfloat16 [8192, 2048], P(('fsdp', 'tp')), may hold values from -6 to 6
- teacher: bfloat16 [8192, 2048], P(('fsdp', 'tp')), may hold values from -6 to 6
- out_grad: bfloat16 [8192, 2048], P(('fsdp', 'tp')), may hold values from -6 to 6
- lengths: int32 [8], P('fsdp'), may hold values from 512 to 1024, as said below
- norm_gain: float32 [2048], P(('fsdp', 'tp')), may hold values from 0.5 to 1.5
- norm_bias: float32 [2048], P(('fsdp', 'tp')), may hold values from -4 to 4
- qkv_weight: bfloat16 [3, 2048, 2048], P(None, 'fsdp', 'tp'), may hold values from -0.125 to 0.125
- qkv_bias: bfloat16 [3, 2048], P(None, ('tp', 'fsdp')), may hold values from -4 to 4
- out_weight: bfloat16 [2048, 2048], P('tp', 'fsdp'), may hold values from -1 to 1
- gate_up_weight: bfloat16 [2, 2048, 5632], P(None, 'fsdp', 'tp'), may hold values from -0.125 to 0.125
- down_weight: bfloat16 [5632, 2048], P('tp', 'fsdp'), may hold values from -0.078125 to 0.078125
Outputs:
- output: bfloat16 [8192, 2048], P(('fsdp', 'tp'))
- loss: float32 [], replicated
- input_grad: bfloat16 [8192, 2048], P(('fsdp', 'tp'))
- norm_gain_grad: float32 [2048], P(('fsdp', 'tp'))
- norm_bias_grad: float32 [2048], P(('fsdp', 'tp'))
- qkv_weight_grad: float32 [3, 2048, 2048], P(None, 'fsdp', 'tp')
- qkv_bias_grad: float32 [3, 2048], P(None, ('tp', 'fsdp'))
- out_weight_grad: float32 [2048, 2048], P('tp', 'fsdp')
- gate_up_weight_grad: float32 [2, 2048, 5632], P(None, 'fsdp', 'tp')
- down_weight_grad: float32 [5632, 2048], P('tp', 'fsdp')
The draws below stay inside these ranges and needn't reach their ends.
Inputs may be any that keep to these rules, and one draw needn't show every extreme that they name: `lengths`: each slot holds at least half of its 1024 positions; some slot is full in every draw.
All inputs are finite; a program needn't handle non-finite values.
Results may differ from the reference program's by a relative error of at most 0.0084.
Values may be sent and summed in bfloat16 or wider, within the bound.
No kernel may reach another device: no remote copies, remote signals or barrier semaphores. Data moves between devices by JAX's collectives and lax.ppermute only.
A program may use at most 256 MiB of HBM per device.

```python
import jax
import jax.numpy as jnp
from jax import lax

D = 2048
H = 32
HD = 64
ROT = 16
FF = 5632
SEQ = 1024
SEQUENCES = 8
TOKENS = 8192


def draw_lengths(key, part):
    drawn_key, place_key = jax.random.split(jax.random.fold_in(key, 7))
    drawn = jax.random.randint(drawn_key, (SEQUENCES,), SEQ // 2, SEQ + 1)
    full_slot = jax.random.randint(place_key, (), 0, SEQUENCES)
    return jnp.where(jnp.arange(SEQUENCES) == full_slot, SEQ, drawn).astype(jnp.int32)


def block_levels(own_key, dims, pieces, least, top_value):
    def one(axis_at, shards_of):
        draws = jax.random.uniform(jax.random.fold_in(jax.random.fold_in(own_key, 6), axis_at), (shards_of,), jnp.float32, least / len(pieces), top_value / len(pieces))
        return jnp.repeat(jnp.exp(draws), dims[axis_at] // shards_of).reshape((-1,) + (1,) * (len(dims) - axis_at - 1))

    loudness = one(*pieces[0])
    for cut in pieces[1:]:
        loudness = loudness * one(*cut)
    return loudness


def noise(rng, extent, deviation, bound, pieces=(), kind=jnp.bfloat16):
    level = block_levels(rng, extent, pieces, -0.22, 0.18) if pieces else 1.0
    array = jax.random.normal(rng, extent, jnp.float32) * deviation * level
    return jnp.minimum(jnp.maximum(array, -bound), bound).astype(kind)


def setup_inputs(seed: int = 0) -> dict:
    keys = jax.random.split(jax.random.key(seed), 12)
    layer_input = noise(keys[0], (TOKENS, D), 1.0, 6.0, ((0, 32),))
    teacher = noise(keys[1], (TOKENS, D), 1.0, 6.0, ((0, 32),))
    out_grad = noise(keys[2], (TOKENS, D), 1.0, 6.0, ((0, 32),))
    lengths = draw_lengths(jax.random.fold_in(keys[11], 71), 0)
    norm_gain = jnp.clip(1.0 + 0.1 * jax.random.normal(keys[4], (D,), jnp.float32), 0.5, 1.5)
    norm_bias = noise(keys[5], (D,), 0.3, 4.0, ((0, 32),), jnp.float32)
    qkv_weight = noise(keys[6], (3, D, D), D ** -0.5, 0.125, ((1, 8), (2, 4)))
    qkv_bias = noise(keys[7], (3, D), 0.3, 4.0, ((1, 32),))
    out_weight = noise(keys[8], (D, D), (D * 16 // SEQ) ** -0.5, 1.0, ((0, 4), (1, 8)))
    gate_up_weight = noise(keys[9], (2, D, FF), D ** -0.5, 0.125, ((1, 8), (2, 4)))
    down_weight = noise(keys[10], (FF, D), FF ** -0.5, 0.078125, ((0, 4), (1, 8)))
    return {"layer_input": layer_input, "teacher": teacher, "out_grad": out_grad, "lengths": lengths, "norm_gain": norm_gain, "norm_bias": norm_bias, "qkv_weight": qkv_weight, "qkv_bias": qkv_bias, "out_weight": out_weight, "gate_up_weight": gate_up_weight, "down_weight": down_weight}


@jax.custom_vjp
def low(v):
    return lax.optimization_barrier(v.astype(jnp.bfloat16)).astype(jnp.float32)

@jax.custom_vjp
def low_back(v):
    return v

def low_keep(v):
    return (low(v), None)

def low_pass(kept, grad):
    return (grad,)

def back_keep(v):
    return (v, None)

def back_low(kept, grad):
    return (low(grad),)
low.defvjp(low_keep, low_pass)
low_back.defvjp(back_keep, back_low)
epsilon = 1e-05
highest = lax.Precision.HIGHEST

def rotary_tables():
    half_rot = ROT // 2
    positions = jnp.arange(SEQ, dtype=jnp.int32).astype(jnp.float32)
    frequency = 10000.0 ** (-2.0 * jnp.arange(half_rot, dtype=jnp.float32) / ROT)
    angles = positions[:, None] * frequency[None, :]
    angles = jnp.concatenate([angles, angles], -1)[:, None, :]
    return (jnp.cos(angles), jnp.sin(angles))

def turn_heads(vectors, cos_tab, sine_tab):
    half_rot = ROT // 2
    head_part = vectors[..., :ROT]
    turned = jnp.concatenate([-head_part[..., half_rot:], head_part[..., :half_rot]], -1)
    return jnp.concatenate([head_part * cos_tab + turned * sine_tab, vectors[..., ROT:]], -1)

def layer(seq_rows, gain_vec, shift_vec, w_qkv, b_qkv, w_out, w_gu, w_down, valid_rows, cos_tab, sine_tab):
    center = seq_rows - lax.optimization_barrier(jnp.mean(seq_rows, -1, keepdims=True))
    spread = lax.optimization_barrier(jnp.mean(center * center, -1, keepdims=True))
    normed = low(center * lax.rsqrt(spread + epsilon) * gain_vec + shift_vec)
    joined_qkv = jnp.einsum('sd,jde->jse', normed, w_qkv, precision=highest) + b_qkv[:, None, :]
    joined_qkv = low_back(joined_qkv)
    queries = low(turn_heads(joined_qkv[0].reshape(SEQ, H, HD), cos_tab, sine_tab))
    key_rows = low(turn_heads(joined_qkv[1].reshape(SEQ, H, HD), cos_tab, sine_tab))
    values = low(joined_qkv[2].reshape(SEQ, H, HD))
    span_rows = min(512, SEQ)
    key_pos = jnp.arange(SEQ, dtype=jnp.int32)

    def attend(row_start):
        q_block = lax.dynamic_slice_in_dim(queries, row_start, span_rows, 0)
        scores = low_back(jnp.einsum('qhe,khe->hqk', q_block, key_rows, precision=highest) * HD ** (-0.5))
        query_pos = row_start + jnp.arange(span_rows, dtype=jnp.int32)
        allowed = key_pos[None, :] <= query_pos[:, None]
        scores = jnp.where(allowed[None], scores, -1e+30)
        shifted = jnp.exp(scores - lax.optimization_barrier(jnp.max(scores, -1, keepdims=True)))
        weights = shifted / lax.optimization_barrier(jnp.sum(shifted, -1, keepdims=True))
        return jnp.einsum('hqk,khe->qhe', low(weights), values, precision=highest)
    starts = jnp.arange(SEQ // span_rows, dtype=jnp.int32) * span_rows
    attended = lax.map(jax.checkpoint(attend), starts).reshape(SEQ, D)
    attended = low(low_back(attended))
    branch_attn = jnp.dot(attended, w_out, precision=highest, preferred_element_type=jnp.float32)
    gate_up = low_back(jnp.einsum('sd,jdf->jsf', normed, w_gu, precision=highest))
    hidden = low(jax.nn.silu(gate_up[0]) * gate_up[1])
    branch_mlp = jnp.dot(hidden, w_down, precision=highest, preferred_element_type=jnp.float32)
    return seq_rows + valid_rows[:, None] * low_back(branch_attn + branch_mlp)

def reference(layer_input, teacher, out_grad, lengths, norm_gain, norm_bias, qkv_weight, qkv_bias, out_weight, gate_up_weight, down_weight):
    params = (norm_gain.astype(jnp.float32), norm_bias.astype(jnp.float32), qkv_weight.astype(jnp.float32), qkv_bias.astype(jnp.float32), out_weight.astype(jnp.float32), gate_up_weight.astype(jnp.float32), down_weight.astype(jnp.float32))
    cos_tab, sine_tab = rotary_tables()
    key_pos = jnp.arange(SEQ, dtype=jnp.int32)
    inputs_all = layer_input.astype(jnp.float32).reshape(SEQUENCES, SEQ, D)
    teacher_all = teacher.astype(jnp.float32).reshape(SEQUENCES, SEQ, D)
    cotangent_all = out_grad.astype(jnp.float32).reshape(SEQUENCES, SEQ, D)

    def one_sequence(state_acc, seq_item):
        seq_rows, target, seed_out, length_one = seq_item
        valid_rows = (key_pos < length_one).astype(jnp.float32)

        def forward(seq_in, *weight_list):
            return layer(seq_in, *weight_list, valid_rows, cos_tab, sine_tab)
        output_rows, pullback = jax.vjp(forward, seq_rows, *params)
        mismatch = output_rows - target
        seed_rows = valid_rows[:, None] * (seed_out + mismatch)
        gradients = pullback(seed_rows)
        totals = tuple((running + fresh for running, fresh in zip(state_acc[0], gradients[1:])))
        squared = jnp.sum(valid_rows[:, None] * mismatch * mismatch)
        return ((totals, state_acc[1] + squared), (output_rows, gradients[0]))
    initial = (tuple((jnp.zeros_like(member) for member in params)), jnp.zeros((), jnp.float32))
    (weight_grads, squared_total), (outputs, input_grads) = lax.scan(one_sequence, initial, (inputs_all, teacher_all, cotangent_all, lengths))
    valid_count = jnp.sum(lengths).astype(jnp.float32)
    loss_value = squared_total / (valid_count * D)
    return (outputs.reshape(TOKENS, D).astype(jnp.bfloat16), loss_value, input_grads.reshape(TOKENS, D).astype(jnp.bfloat16), weight_grads[0], weight_grads[1], weight_grads[2], weight_grads[3], weight_grads[4], weight_grads[5], weight_grads[6])
```

```python
import functools

import jax
import jax.numpy as jnp
from jax import lax
from jax.experimental import pallas as pl
from jax.experimental.pallas import tpu as pltpu
from jax.sharding import Mesh
from jax.sharding import PartitionSpec as P

D = 2048
HD = 64
ROT = 16
SEQ = 1024
PAIR = 2 * HD
SPAN = 256
epsilon = 1e-05
f32 = jnp.float32
bf16 = jnp.bfloat16


def swap_core(a):
    return lax.ppermute(a, "core", [(0, 1), (1, 0)])


def gather_axis(a, axis, n):
    me = lax.axis_index(axis)
    buf = a[None]
    k = 1
    while k < n:
        other = lax.ppermute(buf, axis, [(j, j ^ k) for j in range(n)])
        upper = (me // k) % 2 == 1
        buf = jnp.concatenate(
            [jnp.where(upper, other, buf), jnp.where(upper, buf, other)], 0
        )
        k *= 2
    return buf


def scatter_axis(a, axis, n):
    me = lax.axis_index(axis)
    buf = a
    k = n // 2
    while k >= 1:
        upper = (me // k) % 2 == 1
        lo, hi = buf[:k], buf[k:]
        sent = lax.ppermute(
            jnp.where(upper, lo, hi), axis, [(j, j ^ k) for j in range(n)]
        )
        buf = jnp.where(upper, hi, lo) + sent
        k //= 2
    return buf[0]


def line_gather(piece, n):
    me = lax.axis_index("tp")
    rows = piece.shape[0]
    ups, downs = [], []
    cur = piece
    for s in range(n - 1):
        cur = lax.ppermute(cur, "tp", [(k, k + 1) for k in range(s, n - 1)])
        ups.append(cur)
    cur = piece
    for s in range(n - 1):
        cur = lax.ppermute(cur, "tp", [(k, k - 1) for k in range(1, n - s)])
        downs.append(cur)
    out = jnp.zeros((n * rows,) + piece.shape[1:], piece.dtype)
    for s in reversed(range(n - 1)):
        out = lax.dynamic_update_slice_in_dim(out, ups[s], jnp.maximum(me - 1 - s, 0) * rows, 0)
        out = lax.dynamic_update_slice_in_dim(
            out, downs[s], jnp.minimum(me + 1 + s, n - 1) * rows, 0
        )
    return lax.dynamic_update_slice_in_dim(out, piece, me * rows, 0)


def line_scatter(part, n):
    me = lax.axis_index("tp")
    rows = part.shape[0] // n

    def chunk(j):
        return lax.dynamic_slice_in_dim(part, jnp.clip(j, 0, n - 1) * rows, rows, 0)

    up = down = None
    for s in range(n - 1):
        val = chunk(n - 1 - s + me)
        if up is not None:
            val = val + up.astype(f32)
        up = lax.ppermute(val.astype(bf16), "tp", [(k, k + 1) for k in range(s + 1)])
        val = chunk(s - (n - 1) + me)
        if down is not None:
            val = val + down.astype(f32)
        down = lax.ppermute(
            val.astype(bf16), "tp", [(k, k - 1) for k in range(n - 1 - s, n)]
        )
    return chunk(me) + up.astype(f32) + down.astype(f32)


def rotary_tables():
    half_rot = ROT // 2
    positions = jnp.arange(SEQ, dtype=jnp.int32).astype(f32)
    frequency = 10000.0 ** (-2.0 * jnp.arange(half_rot, dtype=f32) / ROT)
    angles = positions[:, None] * frequency[None, :]
    cos, sin = jnp.cos(angles), jnp.sin(angles)
    rest = HD - ROT
    zero = jnp.zeros((SEQ, rest), f32)
    keep = jnp.concatenate([cos, cos, jnp.ones((SEQ, rest), f32)], -1)
    ahead = jnp.concatenate([-sin, jnp.zeros_like(sin), zero], -1)
    behind = jnp.concatenate([jnp.zeros_like(sin), sin, zero], -1)
    one = jnp.stack([keep, ahead, behind])
    return jnp.concatenate([one, one], -1)


def turned(v, tab_ref, sign):
    half_rot = ROT // 2
    return (
        v * tab_ref[0]
        + sign
        * (
            pltpu.roll(v, PAIR - half_rot, 1) * tab_ref[1]
            + pltpu.roll(v, half_rot, 1) * tab_ref[2]
        )
    )


def dot_nt(a, b):
    return lax.dot_general(a, b, (((1,), (1,)), ((), ())), preferred_element_type=f32)


def dot_nn(a, b):
    return lax.dot_general(a, b, (((1,), (0,)), ((), ())), preferred_element_type=f32)


def dot_tn(a, b):
    return lax.dot_general(a, b, (((0,), (0,)), ((), ())), preferred_element_type=f32)


def own_lanes(a, head):
    lane = lax.broadcasted_iota(jnp.int32, a.shape, 1)
    mine = (lane < HD) if head == 0 else (lane >= HD)
    return jnp.where(mine, a, jnp.zeros_like(a))


def diagonal(span):
    row = lax.broadcasted_iota(jnp.int32, (span, span), 0)
    col = lax.broadcasted_iota(jnp.int32, (span, span), 1)
    return col <= row


def attend_kernel(joined_ref, tab_ref, qkv_ref, attn_ref, lse_ref):
    scale = HD ** (-0.5)
    qkv_ref[0] = (turned(joined_ref[0], tab_ref, 1.0) * scale).astype(bf16)
    qkv_ref[1] = turned(joined_ref[1], tab_ref, 1.0).astype(bf16)
    qkv_ref[2] = joined_ref[2].astype(bf16)
    allowed = diagonal(SPAN)
    lane = lax.broadcasted_iota(jnp.int32, (SPAN, PAIR), 1)
    for i in range(SEQ // SPAN):
        lo, hi = i * SPAN, (i + 1) * SPAN
        q_block = qkv_ref[0, lo:hi, :]
        outs, sums = [], []
        for head in range(2):
            qh = own_lanes(q_block, head)
            near = jnp.where(allowed, dot_nt(qh, qkv_ref[1, lo:hi, :]), -1e30)
            top = jnp.max(near, -1, keepdims=True)
            if i:
                far = dot_nt(qh, qkv_ref[1, 0:lo, :])
                top = jnp.maximum(top, jnp.max(far, -1, keepdims=True))
            near = jnp.exp(near - top)
            total = jnp.sum(near, -1, keepdims=True)
            if i:
                far = jnp.exp(far - top)
                total = total + jnp.sum(far, -1, keepdims=True)
            inverse = 1.0 / total
            out = dot_nn((near * inverse).astype(bf16), qkv_ref[2, lo:hi, :])
            if i:
                out = out + dot_nn((far * inverse).astype(bf16), qkv_ref[2, 0:lo, :])
            outs.append(out)
            sums.append(jnp.broadcast_to(top + jnp.log(total), (SPAN, PAIR)))
        attn_ref[lo:hi, :] = jnp.where(lane < HD, outs[0], outs[1]).astype(bf16)
        lse_ref[lo:hi, :] = jnp.where(lane < HD, sums[0], sums[1])


def attend(joined, tables):
    width = joined.shape[2]
    pairs = width // PAIR
    flops = pairs * 2 * SEQ * SEQ * PAIR * 4
    return pl.pallas_call(
        attend_kernel,
        grid=(pairs,),
        in_specs=[
            pl.BlockSpec((3, SEQ, PAIR), lambda p: (0, 0, p)),
            pl.BlockSpec((3, SEQ, PAIR), lambda p: (0, 0, 0)),
        ],
        out_specs=[
            pl.BlockSpec((3, SEQ, PAIR), lambda p: (0, 0, p)),
            pl.BlockSpec((SEQ, PAIR), lambda p: (0, p)),
            pl.BlockSpec((SEQ, PAIR), lambda p: (0, p)),
        ],
        out_shape=[
            jax.ShapeDtypeStruct((3, SEQ, width), bf16),
            jax.ShapeDtypeStruct((SEQ, width), bf16),
            jax.ShapeDtypeStruct((SEQ, width), f32),
        ],
        compiler_params=pltpu.CompilerParams(vmem_limit_bytes=40 << 20),
        cost_estimate=pl.CostEstimate(
            flops=flops, transcendentals=pairs * SEQ * SEQ, bytes_accessed=24 * SEQ * width
        ),
        name="attend",
    )(joined, tables)


def attend_back_kernel(qkv_ref, grad_ref, lse_ref, tab_ref, out_ref, bias_ref, gk_ref, gv_ref):
    scale = HD ** (-0.5)
    allowed = diagonal(SPAN)
    gk_ref[...] = jnp.zeros_like(gk_ref)
    gv_ref[...] = jnp.zeros_like(gv_ref)
    queries = []
    for i in range(SEQ // SPAN):
        lo, hi = i * SPAN, (i + 1) * SPAN
        gq = jnp.zeros((SPAN, PAIR), f32)
        for head in range(2):
            qh = own_lanes(qkv_ref[0, lo:hi, :], head)
            gh = own_lanes(grad_ref[lo:hi, :], head)
            lse = lse_ref[lo:hi, head * HD : head * HD + 1]
            spans = [(lo, hi, True)] + ([(0, lo, False)] if i else [])
            probs, gprobs = [], []
            inner = jnp.zeros((SPAN, 1), f32)
            for a, b, masked in spans:
                p = jnp.exp(dot_nt(qh, qkv_ref[1, a:b, :]) - lse)
                if masked:
                    p = jnp.where(allowed, p, 0.0)
                g = dot_nt(gh, qkv_ref[2, a:b, :])
                inner = inner + jnp.sum(p * g, -1, keepdims=True)
                probs.append(p)
                gprobs.append(g)
            for (a, b, masked), p, g in zip(spans, probs, gprobs):
                gs = (p * (g - inner)).astype(bf16)
                gk_ref[a:b, :] += dot_tn(gs, qh)
                gv_ref[a:b, :] += dot_tn(p.astype(bf16), gh)
                gq = gq + dot_nn(gs, own_lanes(qkv_ref[1, a:b, :], head))
        queries.append(gq)
    gq = jnp.concatenate(queries, 0) * scale
    for j, g in enumerate((gq, gk_ref[...], gv_ref[...])):
        if j < 2:
            g = turned(g, tab_ref, -1.0)
        g = g.astype(bf16)
        out_ref[j] = g
        bias_ref[j] = jnp.sum(g.astype(f32).reshape(SEQ // 8, 8, PAIR), 0)


def attend_back(qkv, grad, lse, tables):
    width = grad.shape[1]
    pairs = width // PAIR
    flops = pairs * 2 * SEQ * SEQ * PAIR * 10
    return pl.pallas_call(
        attend_back_kernel,
        grid=(pairs,),
        in_specs=[
            pl.BlockSpec((3, SEQ, PAIR), lambda p: (0, 0, p)),
            pl.BlockSpec((SEQ, PAIR), lambda p: (0, p)),
            pl.BlockSpec((SEQ, PAIR), lambda p: (0, p)),
            pl.BlockSpec((3, SEQ, PAIR), lambda p: (0, 0, 0)),
        ],
        out_specs=[
            pl.BlockSpec((3, SEQ, PAIR), lambda p: (0, 0, p)),
            pl.BlockSpec((3, 8, PAIR), lambda p: (0, 0, p)),
        ],
        out_shape=[
            jax.ShapeDtypeStruct((3, SEQ, width), bf16),
            jax.ShapeDtypeStruct((3, 8, width), f32),
        ],
        scratch_shapes=[pltpu.VMEM((SEQ, PAIR), f32), pltpu.VMEM((SEQ, PAIR), f32)],
        compiler_params=pltpu.CompilerParams(vmem_limit_bytes=40 << 20),
        cost_estimate=pl.CostEstimate(
            flops=flops, transcendentals=pairs * SEQ * SEQ, bytes_accessed=20 * SEQ * width
        ),
        name="attend_back",
    )(qkv, grad, lse, tables)


def per_device(
    chips,
    line,
    layer_input,
    teacher,
    out_grad,
    lengths,
    norm_gain,
    norm_bias,
    qkv_weight,
    qkv_bias,
    out_weight,
    gate_up_weight,
    down_weight,
):
    core = lax.axis_index("core")
    place = lax.axis_index("tp")
    rows = layer_input.shape[0]
    feats = D // (2 * chips)
    width = qkv_weight.shape[2]
    dot = functools.partial(jnp.einsum, preferred_element_type=f32)

    def halves(a):
        b = a.reshape(a.shape[:-1] + (chips, 2, feats))
        first, second = b[..., 0, :], b[..., 1, :]
        flat = a.shape[:-1] + (chips * feats,)
        own = jnp.where(core == 0, first, second).reshape(flat)
        other = jnp.where(core == 0, second, first).reshape(flat)
        return own, other

    def whole(own, other):
        flat = own.shape[:-1] + (chips, feats)
        own, other = own.reshape(flat), other.reshape(flat)
        first = jnp.where(core == 0, own, other)
        second = jnp.where(core == 0, other, own)
        return jnp.stack([first, second], -2).reshape(own.shape[:-2] + (D,))

    def weight_halves(w, axis):
        own = lax.all_gather(w, "chip", axis=axis, tiled=True)
        return own, swap_core(own)

    wq = weight_halves(qkv_weight, 1)
    wgu = weight_halves(gate_up_weight, 1)
    wo = weight_halves(out_weight, 1)
    wd = weight_halves(down_weight, 1)

    small = jnp.stack([norm_gain, norm_bias])
    small = gather_axis(small, "tp", line)
    small = small.transpose(1, 0, 2).reshape(2 * feats)
    small = jnp.concatenate([small, qkv_bias.astype(f32).reshape(-1)])
    small = gather_axis(gather_axis(small, "core", 2), "chip", chips)
    small = small.reshape(2 * chips, -1)
    gain = small[:, :feats].reshape(D)
    shift = small[:, feats : 2 * feats].reshape(D)
    bias = small[:, 2 * feats :].reshape(2 * chips, 3, -1)
    bias = bias.transpose(1, 0, 2).reshape(3, width)
    gain_h, shift_h = halves(gain), halves(shift)

    x_own = halves(layer_input)
    x_all = tuple(line_gather(h, line) for h in x_own)

    def moments(xs):
        xs = [h.astype(f32) for h in xs]
        mean = (jnp.sum(xs[0], -1, keepdims=True) + jnp.sum(xs[1], -1, keepdims=True)) / D
        centered = [h - mean for h in xs]
        var = sum(jnp.sum(h * h, -1, keepdims=True) for h in centered) / D
        inv = lax.rsqrt(var + epsilon)
        return mean, inv

    mean, inv_std = moments(x_all)
    unit = [(h.astype(f32) - mean) * inv_std for h in x_all]
    normed = [(u * g + s).astype(bf16) for u, g, s in zip(unit, gain_h, shift_h)]

    joined = dot("sd,jde->jse", normed[0], wq[0]) + dot("sd,jde->jse", normed[1], wq[1])
    joined = joined + bias[:, None, :]
    tables = rotary_tables()
    qkv, attn, lse = attend(joined, tables)
    gate_up = dot("sd,jdf->jsf", normed[0], wgu[0]) + dot("sd,jdf->jsf", normed[1], wgu[1])
    sigmoid = jax.nn.sigmoid(gate_up[0])
    hidden = (gate_up[0] * sigmoid * gate_up[1]).astype(bf16)

    ids = place * rows + jnp.arange(rows, dtype=jnp.int32)
    valid = (ids < lengths[0]).astype(f32)[:, None]
    teach, cot = halves(teacher), halves(out_grad)
    results, seeds, seed_all = [], [], []
    loss_part = jnp.zeros((), f32)
    for h in range(2):
        branch = dot("sa,ad->sd", attn, wo[h]) + dot("sf,fd->sd", hidden, wd[h])
        result = x_own[h].astype(f32) + valid * line_scatter(branch, line)
        mismatch = result - teach[h].astype(f32)
        loss_part = loss_part + jnp.sum(valid * mismatch * mismatch)
        seed = valid * (cot[h].astype(f32) + mismatch)
        results.append(result.astype(bf16))
        seeds.append(seed)
        seed_all.append(line_gather(seed.astype(bf16), line))
    count_part = jnp.sum(valid)

    def weight_grad(make, axis):
        own, other = make(0), make(1)
        both = (own + swap_core(other.astype(bf16)).astype(f32)).astype(bf16)
        return lax.psum_scatter(both, "chip", scatter_dimension=axis, tiled=True).astype(f32)

    down_grad = weight_grad(lambda h: dot("sf,sd->fd", hidden, seed_all[h]), 1)
    out_w_grad = weight_grad(lambda h: dot("sa,sd->ad", attn, seed_all[h]), 1)
    grad_attn = (
        dot("sd,ad->sa", seed_all[0], wo[0]) + dot("sd,ad->sa", seed_all[1], wo[1])
    ).astype(bf16)
    grad_qkv, grad_bias = attend_back(qkv, grad_attn, lse, tables)
    grad_hidden = dot("sd,fd->sf", seed_all[0], wd[0]) + dot("sd,fd->sf", seed_all[1], wd[1])
    grad_gate = grad_hidden * gate_up[1] * sigmoid * (1.0 + gate_up[0] * (1.0 - sigmoid))
    grad_up = grad_hidden * gate_up[0] * sigmoid
    grad_gu = jnp.stack([grad_gate, grad_up]).astype(bf16)
    gu_grad = weight_grad(lambda h: dot("sd,jsf->jdf", normed[h], grad_gu), 1)
    qkv_grad = weight_grad(lambda h: dot("sd,jse->jde", normed[h], grad_qkv), 1)

    grad_normed, gain_parts, shift_parts = [], [], []
    for h in range(2):
        part = dot("jse,jde->sd", grad_qkv, wq[h]) + dot("jsf,jdf->sd", grad_gu, wgu[h])
        gain_parts.append(jnp.sum(part * unit[h], 0))
        shift_parts.append(jnp.sum(part, 0))
        grad_normed.append(line_scatter(part, line))

    mean, inv_std = moments(x_own)
    unit = [(h.astype(f32) - mean) * inv_std for h in x_own]
    grad_unit = [g * w for g, w in zip(grad_normed, gain_h)]
    m1 = sum(jnp.sum(g, -1, keepdims=True) for g in grad_unit) / D
    m2 = sum(jnp.sum(g * u, -1, keepdims=True) for g, u in zip(grad_unit, unit)) / D
    input_grad = [
        (s + inv_std * (g - m1 - u * m2)).astype(bf16)
        for s, g, u in zip(seeds, grad_unit, unit)
    ]

    scalars = jnp.stack([loss_part, count_part])
    vectors = jnp.stack([whole(*gain_parts), whole(*shift_parts)])
    vectors = vectors.reshape(2, chips, 2, line, -1).transpose(1, 2, 3, 0, 4)
    vectors = vectors.reshape(chips, 2, line, -1)
    vectors = jnp.concatenate(
        [vectors, jnp.broadcast_to(scalars, (chips, 2, line, 2))], -1
    ).reshape(chips, 2, -1)
    heads = jnp.sum(grad_bias, 1).reshape(3, chips, 2, -1).transpose(1, 2, 0, 3)
    heads = heads.reshape(chips, 2, -1)
    sums = jnp.concatenate([vectors, heads], -1)
    sums = scatter_axis(scatter_axis(sums, "chip", chips), "core", 2)
    qkv_b_grad = sums[vectors.shape[-1] :].reshape(3, -1)
    sums = scatter_axis(sums[: vectors.shape[-1]].reshape(line, -1), "tp", line)
    n = norm_gain.shape[0]
    gain_grad, bias_grad = sums[:n], sums[n : 2 * n]
    loss_value = sums[2 * n] / (sums[2 * n + 1] * D)
    return (
        whole(*results),
        loss_value,
        whole(*input_grad),
        gain_grad,
        bias_grad,
        qkv_grad,
        qkv_b_grad,
        out_w_grad,
        gu_grad,
        down_grad,
    )


def solution(mesh):
    chips, line = mesh.shape["fsdp"] // 2, mesh.shape["tp"]
    fine = Mesh(mesh.devices.reshape(chips, 2, line), ("chip", "core", "tp"))
    fsdp = ("chip", "core")
    tokens = P(fsdp + ("tp",), None)
    vector = P(fsdp + ("tp",))
    return jax.shard_map(
        functools.partial(per_device, chips, line),
        mesh=fine,
        in_specs=(
            tokens,
            tokens,
            tokens,
            P(fsdp),
            vector,
            vector,
            P(None, fsdp, "tp"),
            P(None, ("tp",) + fsdp),
            P("tp", fsdp),
            P(None, fsdp, "tp"),
            P("tp", fsdp),
        ),
        out_specs=(
            tokens,
            P(),
            tokens,
            vector,
            vector,
            P(None, fsdp, "tp"),
            P(None, ("tp",) + fsdp),
            P("tp", fsdp),
            P(None, fsdp, "tp"),
            P("tp", fsdp),
        ),
        check_vma=False,
    )
```

```python
import functools

import jax
import jax.numpy as jnp
from jax import lax
from jax.experimental import pallas as pl
from jax.experimental.pallas import tpu as pltpu
from jax.sharding import Mesh
from jax.sharding import PartitionSpec as P

D = 2048
HD = 64
ROT = 16
SEQ = 1024
PAIR = 2 * HD
SPAN = 256
epsilon = 1e-05
f32 = jnp.float32
bf16 = jnp.bfloat16


def after(value, *others):
    return lax.optimization_barrier((value,) + others)[0]


def swap_core(a):
    return lax.ppermute(a, "core", [(0, 1), (1, 0)])


def gather_axis(a, axis, n):
    me = lax.axis_index(axis)
    buf = a[None]
    k = 1
    while k < n:
        other = lax.ppermute(buf, axis, [(j, j ^ k) for j in range(n)])
        upper = (me // k) % 2 == 1
        buf = jnp.concatenate(
            [jnp.where(upper, other, buf), jnp.where(upper, buf, other)], 0
        )
        k *= 2
    return buf


def scatter_axis(a, axis, n):
    me = lax.axis_index(axis)
    buf = a
    k = n // 2
    while k >= 1:
        upper = (me // k) % 2 == 1
        lo, hi = buf[:k], buf[k:]
        sent = lax.ppermute(
            jnp.where(upper, lo, hi), axis, [(j, j ^ k) for j in range(n)]
        )
        buf = jnp.where(upper, hi, lo) + sent
        k //= 2
    return buf[0]


def line_scatter(part, n, holds=()):
    me = lax.axis_index("tp")
    rows = part.shape[0] // n

    def chunk(j):
        return lax.dynamic_slice_in_dim(part, jnp.clip(j, 0, n - 1) * rows, rows, 0)

    def plus(a, b):
        return a if b is None else (a.astype(f32) + b.astype(f32)).astype(bf16)

    up = down = None
    for s in range(n - 1):
        up = plus(chunk(n - 1 - s + me), up)
        down = plus(chunk(s - (n - 1) + me), down)
        up = lax.ppermute(up, "tp", [(k, k + 1) for k in range(s + 1)])
        down = lax.ppermute(down, "tp", [(k, k - 1) for k in range(n - 1 - s, n)])
        if s < len(holds):
            up, down = after(up, holds[s]), after(down, holds[s])
    return chunk(me).astype(f32) + up.astype(f32) + down.astype(f32)


def rotary_tables(line):
    half_rot = ROT // 2
    positions = jnp.arange(SEQ, dtype=jnp.int32).astype(f32)
    frequency = 10000.0 ** (-2.0 * jnp.arange(half_rot, dtype=f32) / ROT)
    angles = positions[:, None] * frequency[None, :]
    cos, sin = jnp.cos(angles), jnp.sin(angles)
    rest = HD - ROT
    zero = jnp.zeros((SEQ, rest), f32)
    keep = jnp.concatenate([cos, cos, jnp.ones((SEQ, rest), f32)], -1)
    ahead = jnp.concatenate([-sin, jnp.zeros_like(sin), zero], -1)
    behind = jnp.concatenate([jnp.zeros_like(sin), sin, zero], -1)
    one = jnp.stack([keep, ahead, behind])
    one = jnp.concatenate([one, one], -1).reshape(3, line, 2, -1, PAIR)
    return [one[:, :, t].reshape(3, SEQ // 2, PAIR) for t in range(2)]


def turned(v, tab_ref, sign):
    half_rot = ROT // 2
    return (
        v * tab_ref[0]
        + sign
        * (
            pltpu.roll(v, PAIR - half_rot, 1) * tab_ref[1]
            + pltpu.roll(v, half_rot, 1) * tab_ref[2]
        )
    )


def dot_nt(a, b):
    return lax.dot_general(a, b, (((1,), (1,)), ((), ())), preferred_element_type=f32)


def dot_nn(a, b):
    return lax.dot_general(a, b, (((1,), (0,)), ((), ())), preferred_element_type=f32)


def dot_tn(a, b):
    return lax.dot_general(a, b, (((0,), (0,)), ((), ())), preferred_element_type=f32)


def two_heads(a):
    lane = lax.broadcasted_iota(jnp.int32, a.shape, 1)
    zero = jnp.zeros_like(a)
    return jnp.concatenate([jnp.where(lane < HD, a, zero), jnp.where(lane < HD, zero, a)], 0)


def one_row_each(a):
    rows = a.shape[1] // 2
    dim = lax.broadcasted_iota(jnp.int32, (PAIR, rows), 0)
    return jnp.where(dim < HD, a[:, :rows], a[:, rows:]).T


def spans(part, z, span):
    return ((z + 1) * span, (z + part) * span)


def masked(a, span, fill):
    lo = a.shape[0] - span
    key = lax.broadcasted_iota(jnp.int32, (span, 2 * span), 0)
    query = lax.broadcasted_iota(jnp.int32, (span, 2 * span), 1)
    query = jnp.where(query >= span, query - span, query)
    tail = jnp.where(key <= query, a[lo:], fill)
    return jnp.concatenate([a[:lo], tail], 0) if lo else tail


def attend_kernel(part, span, q_ref, k0_ref, v0_ref, k1_ref, v1_ref, attn_ref, lse_ref):
    keys, values = (k0_ref, k1_ref), (v0_ref[0].T, v1_ref[0].T)
    for z in range(SEQ // 2 // span):
        rows = slice(z * span, (z + 1) * span)
        q = two_heads(q_ref[0, rows, :])
        scores = {}
        for t, count in enumerate(spans(part, z, span)):
            if count:
                scores[t] = dot_nt(keys[t][0, :count, :], q)
        scores[part] = masked(scores[part], span, -1e30)
        top = functools.reduce(
            jnp.maximum, [jnp.max(a, 0, keepdims=True) for a in scores.values()]
        )
        scores = {t: jnp.exp(a - top) for t, a in scores.items()}
        total = sum(jnp.sum(a, 0, keepdims=True) for a in scores.values())
        inverse = 1.0 / total
        out = sum(
            dot_nn(values[t][:, : a.shape[0]], (a * inverse).astype(bf16))
            for t, a in scores.items()
        )
        attn_ref[rows, :] = one_row_each(out).astype(bf16)
        lse_ref[0, z : z + 1, :] = top + jnp.log(total)


def head_spec(j):
    return pl.BlockSpec((1, SEQ // 2, PAIR), lambda p: (j, 0, p))


def attend(part, span, qkv):
    width = qkv[0].shape[2]
    pairs = width // PAIR
    blocks = SEQ // 2 // span
    half = SEQ // 2
    mine = pl.BlockSpec((half, PAIR), lambda p: (0, p))
    return pl.pallas_call(
        functools.partial(attend_kernel, part, span),
        grid=(pairs,),
        in_specs=[head_spec(0), head_spec(1), head_spec(2), head_spec(1), head_spec(2)],
        out_specs=[mine, pl.BlockSpec((1, blocks, 2 * span), lambda p: (p, 0, 0))],
        out_shape=[
            jax.ShapeDtypeStruct((half, width), bf16),
            jax.ShapeDtypeStruct((pairs, blocks, 2 * span), f32),
        ],
        compiler_params=pltpu.CompilerParams(vmem_limit_bytes=30 << 20),
        cost_estimate=pl.CostEstimate(
            flops=pairs * SEQ * SEQ * PAIR * 4,
            transcendentals=pairs * SEQ * SEQ,
            bytes_accessed=10 * SEQ * width,
        ),
        name="attend",
    )(qkv[part], qkv[0], qkv[0], qkv[1], qkv[1])


def attend_back_kernel(
    part, span, q_ref, k0_ref, v0_ref, k1_ref, v1_ref, grad_ref, lse_ref, tab0_ref, tab1_ref, *refs
):
    scale = HD ** (-0.5)
    half = SEQ // 2
    if part == 0:
        gq_ref, *gkv_refs = refs
        sums = gkv_refs
        for ref in sums:
            ref[...] = jnp.zeros_like(ref)
    else:
        gq0_ref, *kept = refs[:5]
        out_ref, bias_ref, gq_ref, *sums = refs[5:]
        for ref, old in zip(sums, kept):
            ref[...] = old[...]
    keys, values = (k0_ref, k1_ref), (v0_ref, v1_ref)
    turned_keys = (k0_ref[0].T, k1_ref[0].T)
    for z in range(half // span):
        rows = slice(z * span, (z + 1) * span)
        q, g = two_heads(q_ref[0, rows, :]), two_heads(grad_ref[rows, :])
        lse = lse_ref[0, z : z + 1, :]
        probs, gprobs = {}, {}
        inner = 0.0
        for t, count in enumerate(spans(part, z, span)):
            if count:
                p = jnp.exp(dot_nt(keys[t][0, :count, :], q) - lse)
                probs[t] = masked(p, span, 0.0) if t == part else p
                gprobs[t] = dot_nt(values[t][0, :count, :], g)
                inner = inner + jnp.sum(probs[t] * gprobs[t], 0, keepdims=True)
        gq = 0.0
        for t, p in probs.items():
            count = p.shape[0]
            gs = (p * (gprobs[t] - inner)).astype(bf16)
            sums[2 * t][:count, :] += dot_nn(gs, q)
            sums[2 * t + 1][:count, :] += dot_nn(p.astype(bf16), g)
            gq = gq + dot_nn(turned_keys[t][:, :count], gs)
        gq_ref[rows, :] = one_row_each(gq) * scale
    if part == 1:
        pairs = pl.num_programs(0)
        pair = pl.program_id(0)
        for j in range(3):
            lanes = pl.ds(pl.multiple_of((j * pairs + pair) * PAIR, PAIR), PAIR)
            bias = 0.0
            for t, tab_ref in enumerate((tab0_ref, tab1_ref)):
                g = sums[2 * t + j - 1][...] if j else (gq_ref if t else gq0_ref)[...]
                if j < 2:
                    g = turned(g, tab_ref, -1.0)
                g = g.astype(bf16)
                out_ref[t * half : (t + 1) * half, lanes] = g
                bias = bias + jnp.sum(g.astype(f32).reshape(half // 8, 8, PAIR), 0)
            bias_ref[:, lanes] = bias


def attend_back(part, span, qkv, grad, lse, tables, kept=()):
    width = grad.shape[1]
    pairs = width // PAIR
    blocks = SEQ // 2 // span
    half = SEQ // 2
    mine = pl.BlockSpec((half, PAIR), lambda p: (0, p))
    table = pl.BlockSpec((3, half, PAIR), lambda p: (0, 0, 0))
    partial_shapes = [jax.ShapeDtypeStruct((half, width), f32)] * 5
    if part == 0:
        out_specs, out_shape, scratch = [mine] * 5, partial_shapes, []
    else:
        out_specs = [
            pl.BlockSpec((SEQ, 3 * width), lambda p: (0, 0)),
            pl.BlockSpec((8, 3 * width), lambda p: (0, 0)),
        ]
        out_shape = [
            jax.ShapeDtypeStruct((SEQ, 3 * width), bf16),
            jax.ShapeDtypeStruct((8, 3 * width), f32),
        ]
        scratch = [pltpu.VMEM((half, PAIR), f32)] * 5
    return pl.pallas_call(
        functools.partial(attend_back_kernel, part, span),
        grid=(pairs,),
        in_specs=[head_spec(0), head_spec(1), head_spec(2), head_spec(1), head_spec(2)]
        + [mine, pl.BlockSpec((1, blocks, 2 * span), lambda p: (p, 0, 0)), table, table]
        + [mine] * len(kept),
        out_specs=out_specs,
        out_shape=out_shape,
        scratch_shapes=scratch,
        compiler_params=pltpu.CompilerParams(vmem_limit_bytes=30 << 20),
        cost_estimate=pl.CostEstimate(
            flops=pairs * SEQ * SEQ * PAIR * 10,
            transcendentals=pairs * SEQ * SEQ,
            bytes_accessed=20 * SEQ * width,
        ),
        name="attend_back",
    )(qkv[part], qkv[0], qkv[0], qkv[1], qkv[1], grad, lse, *tables, *kept)


def call(kernel, name, grid, in_specs, out_specs, out_shape, scalars, args, flops=0, scratch=()):
    moved = sum(a.size * a.dtype.itemsize for a in args)
    moved += sum(o.size * jnp.dtype(o.dtype).itemsize for o in out_shape)
    return pl.pallas_call(
        kernel,
        grid_spec=pltpu.PrefetchScalarGridSpec(
            num_scalar_prefetch=1,
            grid=grid,
            in_specs=in_specs,
            out_specs=out_specs,
            scratch_shapes=scratch,
        ),
        out_shape=out_shape,
        compiler_params=pltpu.CompilerParams(vmem_limit_bytes=30 << 20),
        cost_estimate=pl.CostEstimate(flops=flops, transcendentals=0, bytes_accessed=moved),
        name=name,
    )(scalars, *args)


def whole_spec(shape):
    zeros = (0,) * len(shape)
    return pl.BlockSpec(shape, lambda i, s: zeros, pipeline_mode=pl.Buffered(1))


def shard_spec(w):
    rest = (0,) * (w.ndim - 1)
    return pl.BlockSpec((1,) + w.shape[1:], lambda k, s: (k,) + rest)


def all_spec(rows, cols):
    return pl.BlockSpec((rows, cols), lambda k, s: (0, 0), pipeline_mode=pl.Buffered(1))


def over_rows(rows, step, body):
    @pl.loop(0, rows // step)
    def _(i):
        body(pl.ds(pl.multiple_of(i * step, step), step))


def row_spec(rows, cols):
    return pl.BlockSpec((rows, cols), lambda i, s: (i, 0))


def shape_of(shape, dtype):
    return jax.ShapeDtypeStruct(shape, dtype)


def lanes_of(scalar_ref, h, p, feats):
    block = 2 * p + jnp.bitwise_xor(scalar_ref[0], h)
    return pl.ds(pl.multiple_of(block * feats, feats), feats)


def shard_lanes(scalar_ref, k, feats, first=0):
    block = jnp.bitwise_xor(scalar_ref[1], k)
    return pl.ds(pl.multiple_of(first + block * feats, feats), feats)


def moments(x):
    mean = jnp.sum(x, -1, keepdims=True) / D
    x = x - mean
    return mean, lax.rsqrt(jnp.sum(x * x, -1, keepdims=True) / D + epsilon)


def norm_kernel(feats, s_ref, x_ref, vec_ref, own_ref, other_ref, stat_ref, copy_ref):
    mean, inv = moments(x_ref[...].astype(f32))
    copy_ref[...] = x_ref[...]
    for h, out_ref in enumerate((own_ref, other_ref)):
        for p in range(D // (2 * feats)):
            at = lanes_of(s_ref, h, p, feats)
            u = (x_ref[:, at].astype(f32) - mean) * inv
            out_ref[:, p * feats : (p + 1) * feats] = (
                u * vec_ref[0:1, at] + vec_ref[1:2, at]
            ).astype(bf16)
    lane = lax.broadcasted_iota(jnp.int32, stat_ref.shape, 1)
    stat_ref[...] = jnp.where(lane < PAIR // 2, mean, inv)


def norm(scalars, part, span, x, vectors, feats):
    half = D // 2
    rows = SEQ // 2
    return call(
        functools.partial(norm_kernel, feats),
        "norm",
        (rows // span,),
        [pl.BlockSpec((span, D), lambda z, s: (2 * z + part, 0)), whole_spec((2, D))],
        [row_spec(span, half), row_spec(span, half), row_spec(span, PAIR), row_spec(span, D)],
        [shape_of((rows, half), bf16)] * 2
        + [shape_of((rows, PAIR), f32), shape_of((rows, D), bf16)],
        scalars,
        (x, vectors),
    )


def joined_kernel(
    s_ref, own_ref, other_ref, bias_ref, tab_ref, w0_ref, w1_ref, out_ref, sum_ref
):
    _, many, feats, width = w0_ref.shape
    k, last_k = pl.program_id(0), pl.num_programs(0) - 1
    at = shard_lanes(s_ref, k, feats)
    rows = own_ref.shape[0]

    @pl.when(k == 0)
    def _():
        for j in range(many):
            sum_ref[j] = jnp.broadcast_to(bias_ref[j], (rows, width))

    def step(here):
        x0, x1 = own_ref[here, at], other_ref[here, at]
        for j in range(many):
            sum_ref[j, here, :] += dot_nn(x0, w0_ref[0, j]) + dot_nn(x1, w1_ref[0, j])

    over_rows(rows, SPAN, step)

    @pl.when(k == last_k)
    def _():
        def rotate(here):
            tab = tab_ref[:, here, :]
            for j in range(2):
                scale = 1.0 if j else HD ** (-0.5)
                for p in range(width // PAIR):
                    lanes = slice(p * PAIR, (p + 1) * PAIR)
                    out_ref[j, here, lanes] = (
                        turned(sum_ref[j, here, lanes], tab, 1.0) * scale
                    ).astype(bf16)
            out_ref[2, here, :] = sum_ref[2, here, :].astype(bf16)

        over_rows(rows, 64, rotate)


def joined_heads(scalars, normed, weights, bias, table):
    chips, many, _, width = weights[0].shape
    rows = normed[0].shape[0]
    return call(
        joined_kernel,
        "joined",
        (chips,),
        [all_spec(rows, D // 2)] * 2
        + [whole_spec((3, 1, width)), whole_spec((3, rows, PAIR))]
        + [shard_spec(w) for w in weights],
        [pl.BlockSpec((3, rows, width), lambda k, s: (0, 0, 0))],
        [shape_of((3, rows, width), bf16)],
        scalars,
        (*normed, bias, table, *weights),
        flops=2 * rows * D * 3 * width,
        scratch=[pltpu.VMEM((many, rows, width), f32)],
    )[0]


def gate_up_kernel(
    s_ref, own_ref, other_ref, attn_ref, w0_ref, w1_ref, gate_ref, up_ref, acts_ref
):
    width = attn_ref.shape[1]
    feats = w0_ref.shape[2]
    k, last_k = pl.program_id(0), pl.num_programs(0) - 1
    at = shard_lanes(s_ref, k, feats)
    rows = own_ref.shape[0]

    @pl.when(k == 0)
    def _():
        gate_ref[...] = jnp.zeros_like(gate_ref)
        up_ref[...] = jnp.zeros_like(up_ref)
        acts_ref[:, :width] = attn_ref[...]

    def step(here):
        x0, x1 = own_ref[here, at], other_ref[here, at]
        for j, out_ref in enumerate((gate_ref, up_ref)):
            out_ref[here, :] += dot_nn(x0, w0_ref[0, j]) + dot_nn(x1, w1_ref[0, j])

    over_rows(rows, SPAN, step)

    @pl.when(k == last_k)
    def _():
        def join(here):
            gate = gate_ref[here, :]
            acts_ref[here, width:] = (gate * jax.nn.sigmoid(gate) * up_ref[here, :]).astype(bf16)

        over_rows(rows, 64, join)


def gate_up(scalars, normed, attn, weights):
    chips, _, _, hid = weights[0].shape
    rows, width = attn.shape
    return call(
        gate_up_kernel,
        "gate_up",
        (chips,),
        [all_spec(rows, D // 2)] * 2
        + [all_spec(rows, width)]
        + [shard_spec(w) for w in weights],
        [all_spec(rows, hid), all_spec(rows, hid), all_spec(rows, width + hid)],
        [shape_of((rows, hid), f32)] * 2 + [shape_of((rows, width + hid), bf16)],
        scalars,
        (*normed, attn, *weights),
        flops=4 * rows * D * hid,
    )


def branch_kernel(s_ref, acts_ref, w0_ref, w1_ref, out_ref):
    feats = w0_ref.shape[2]
    p = pl.program_id(0)
    rows = acts_ref.shape[0]

    def step(here):
        acts = acts_ref[here, :]
        for h, w_ref in enumerate((w0_ref, w1_ref)):
            at = pl.ds(pl.multiple_of(h * D // 2 + p * feats, feats), feats)
            out_ref[here, at] = dot_nn(acts, w_ref[0]).astype(bf16)

    over_rows(rows, SPAN, step)


def branch_sums(scalars, acts, weights):
    chips = weights[0].shape[0]
    rows, deep = acts.shape
    return call(
        branch_kernel,
        "branch",
        (chips,),
        [all_spec(rows, deep)] + [shard_spec(w) for w in weights],
        [all_spec(rows, D)],
        [shape_of((rows, D), bf16)],
        scalars,
        (acts, *weights),
        flops=2 * rows * deep * D,
    )[0]


def finish_kernel(
    feats, part, s_ref, branch_ref, x_ref, teach_ref, cot_ref, old_ref,
    result_ref, seed_ref, low_ref, loss_ref,
):
    rows = x_ref.shape[0]
    first = (2 * s_ref[2] + part) * rows
    valid = (first + lax.broadcasted_iota(jnp.int32, (rows, 1), 0) < s_ref[3]).astype(f32)
    loss = jnp.zeros((8, PAIR), f32)
    chips = D // (2 * feats)
    for h in range(2):
        for k in range(chips):
            at = lanes_of(s_ref, h, k, feats)
            here = slice((h * chips + k) * feats, (h * chips + k + 1) * feats)
            y = x_ref[:, at].astype(f32) + valid * branch_ref[:, here].astype(f32)
            mismatch = y - teach_ref[:, at].astype(f32)
            square = jnp.sum((valid * mismatch * mismatch).reshape(rows // 8, 8, feats), 0)
            for q in range(feats // PAIR):
                loss = loss + square[:, q * PAIR : (q + 1) * PAIR]
            seed = valid * (cot_ref[:, at].astype(f32) + mismatch)
            result_ref[:, at] = y.astype(bf16)
            seed_ref[:, at] = seed
            low_ref[:, here] = seed.astype(bf16)
    loss_ref[...] = loss


def part_spec(rows, cols, part):
    return pl.BlockSpec((rows, cols), lambda i, s: (part, 0))


def aliased(kernel, name, in_specs, out_specs, out_shape, scalars, args, aliases):
    moved = sum(o.size * jnp.dtype(o.dtype).itemsize for o in out_shape)
    return pl.pallas_call(
        kernel,
        grid_spec=pltpu.PrefetchScalarGridSpec(
            num_scalar_prefetch=1, grid=(1,), in_specs=in_specs, out_specs=out_specs
        ),
        out_shape=out_shape,
        input_output_aliases=aliases,
        compiler_params=pltpu.CompilerParams(vmem_limit_bytes=24 << 20),
        cost_estimate=pl.CostEstimate(flops=0, transcendentals=0, bytes_accessed=3 * moved),
        name=name,
    )(scalars, *args)


def finish(scalars, part, branch, x, teacher, out_grad, old, feats):
    rows = branch.shape[0]
    mine = part_spec(rows, D, part)
    one = part_spec(rows, D, 0)
    aliases = {}
    if old is None:
        old = jnp.zeros((8, PAIR), bf16)
        old_spec = part_spec(8, PAIR, 0)
    else:
        old_spec = pl.BlockSpec(memory_space=pl.ANY)
        aliases = {5: 0}
    return aliased(
        functools.partial(finish_kernel, feats, part),
        "finish",
        [one, mine, mine, mine, old_spec],
        [mine, one, one, part_spec(8, PAIR, 0)],
        [
            shape_of((2 * rows, D), bf16),
            shape_of((rows, D), f32),
            shape_of((rows, D), bf16),
            shape_of((8, PAIR), f32),
        ],
        scalars,
        (branch, x, teacher, out_grad, old),
        aliases,
    )


def grad_acts_kernel(
    s_ref, seed_ref, gate_ref, up_ref, w0_ref, w1_ref, attn_ref, gu_ref, sum_ref
):
    hid = gate_ref.shape[1]
    width = attn_ref.shape[1]
    feats = w0_ref.shape[2]
    p, last_p = pl.program_id(0), pl.num_programs(0) - 1
    rows = seed_ref.shape[0]

    @pl.when(p == 0)
    def _():
        sum_ref[...] = jnp.zeros_like(sum_ref)

    def step(here):
        total = sum_ref[here, :]
        for h, w_ref in enumerate((w0_ref, w1_ref)):
            at = pl.ds(pl.multiple_of(h * D // 2 + p * feats, feats), feats)
            total = total + dot_nt(seed_ref[here, at], w_ref[0])
        sum_ref[here, :] = total

    over_rows(rows, SPAN, step)

    @pl.when(p == last_p)
    def _():
        def split(here):
            attn_ref[here, :] = sum_ref[here, :width].astype(bf16)
            grad = sum_ref[here, width:]
            gate, up = gate_ref[here, :], up_ref[here, :]
            sigmoid = jax.nn.sigmoid(gate)
            gu_ref[here, :hid] = (
                grad * up * sigmoid * (1.0 + gate * (1.0 - sigmoid))
            ).astype(bf16)
            gu_ref[here, hid:] = (grad * gate * sigmoid).astype(bf16)

        over_rows(rows, 64, split)


def grad_acts(scalars, seed, weights, gate, up):
    chips, deep, _ = weights[0].shape
    rows, hid = gate.shape
    width = deep - hid
    return call(
        grad_acts_kernel,
        "grad_acts",
        (chips,),
        [all_spec(rows, D), all_spec(rows, hid), all_spec(rows, hid)]
        + [shard_spec(w) for w in weights],
        [all_spec(rows, width), all_spec(rows, 2 * hid)],
        [shape_of((rows, width), bf16), shape_of((rows, 2 * hid), bf16)],
        scalars,
        (seed, gate, up, *weights),
        flops=2 * rows * D * deep,
        scratch=[pltpu.VMEM((rows, deep), f32)],
    )


def grad_normed_kernel(s_ref, qkv_ref, gu_ref, x_ref, stat_ref, *refs):
    w_refs, (out_ref, gain_ref, shift_ref) = refs[:4], refs[4:]
    feats = w_refs[0].shape[2]
    k = pl.program_id(0)
    rows = x_ref.shape[0]
    at = [shard_lanes(s_ref, k, feats, h * D // 2) for h in range(2)]
    for h in range(2):
        gain_ref[:, at[h]] = jnp.zeros((8, feats), f32)
        shift_ref[:, at[h]] = jnp.zeros((8, feats), f32)

    def step(here):
        mean, inv = stat_ref[here, 0:1], stat_ref[here, PAIR // 2 : PAIR // 2 + 1]
        for h in range(2):
            g = 0.0
            for a_ref, w_ref in ((qkv_ref, w_refs[h]), (gu_ref, w_refs[2 + h])):
                _, many, _, wide = w_ref.shape
                for j in range(many):
                    g = g + dot_nt(a_ref[here, j * wide : (j + 1) * wide], w_ref[0, j])
            out_ref[here, at[h]] = g.astype(bf16)
            lanes = lanes_of(s_ref, h, jnp.bitwise_xor(s_ref[1], k), feats)
            u = (x_ref[here, lanes].astype(f32) - mean) * inv
            gain_ref[:, at[h]] += jnp.sum((g * u).reshape(-1, 8, feats), 0)
            shift_ref[:, at[h]] += jnp.sum(g.reshape(-1, 8, feats), 0)

    over_rows(rows, SPAN, step)


def grad_normed(scalars, part, grad_qkv, grad_gu, w_qkv, w_gu, x, stats):
    chips, _, _, width = w_qkv[0].shape
    hid = w_gu[0].shape[3]
    rows = x.shape[0]
    weights = (*w_qkv, *w_gu)
    return call(
        grad_normed_kernel,
        "grad_normed",
        (chips,),
        [
            pl.BlockSpec((rows, 3 * width), lambda k, s: (part, 0)),
            all_spec(rows, 2 * hid),
            all_spec(rows, D),
            all_spec(rows, PAIR),
        ]
        + [shard_spec(w) for w in weights],
        [all_spec(rows, D), all_spec(8, D), all_spec(8, D)],
        [shape_of((rows, D), bf16), shape_of((8, D), f32), shape_of((8, D), f32)],
        scalars,
        (grad_qkv, grad_gu, x, stats, *weights),
        flops=2 * rows * D * (3 * width + 2 * hid),
    )


def last_kernel(feats, s_ref, sum_ref, x_ref, vec_ref, seed_ref, old_ref, out_ref):
    mean, inv = moments(x_ref[...].astype(f32))
    chips = D // (2 * feats)

    def units(h, k):
        here = slice((h * chips + k) * feats, (h * chips + k + 1) * feats)
        at = lanes_of(s_ref, h, k, feats)
        g = sum_ref[:, here].astype(f32) * vec_ref[0:1, at]
        return g, (x_ref[:, at].astype(f32) - mean) * inv, at

    m1 = m2 = 0.0
    for h in range(2):
        for k in range(chips):
            g, u, _ = units(h, k)
            m1 = m1 + jnp.sum(g, -1, keepdims=True)
            m2 = m2 + jnp.sum(g * u, -1, keepdims=True)
    m1, m2 = m1 / D, m2 / D
    for h in range(2):
        for k in range(chips):
            g, u, at = units(h, k)
            out_ref[:, at] = (seed_ref[:, at] + inv * (g - m1 - u * m2)).astype(bf16)


def last(scalars, part, total, x, vectors, seed, old, feats):
    rows = total.shape[0]
    mine = part_spec(rows, D, part)
    one = part_spec(rows, D, 0)
    aliases = {}
    if old is None:
        old = jnp.zeros((8, PAIR), bf16)
        old_spec = part_spec(8, PAIR, 0)
    else:
        old_spec = pl.BlockSpec(memory_space=pl.ANY)
        aliases = {5: 0}
    return aliased(
        functools.partial(last_kernel, feats),
        "last",
        [one, mine, part_spec(2, D, 0), one, old_spec],
        [mine],
        [shape_of((2 * rows, D), bf16)],
        scalars,
        (total, x, vectors, seed, old),
        aliases,
    )[0]


def per_device(
    chips,
    line,
    layer_input,
    teacher,
    out_grad,
    lengths,
    norm_gain,
    norm_bias,
    qkv_weight,
    qkv_bias,
    out_weight,
    gate_up_weight,
    down_weight,
):
    core = lax.axis_index("core")
    chip = lax.axis_index("chip")
    place = lax.axis_index("tp")
    scalars = jnp.stack([core, chip, place, lengths[0]]).astype(jnp.int32)
    feats = D // (2 * chips)
    width = qkv_weight.shape[2]
    hid = down_weight.shape[0]
    n = norm_gain.shape[0]
    cat = jnp.concatenate

    def to_chip(a, k):
        return lax.ppermute(a, "chip", [(c, c ^ k) for c in range(chips)])

    def near_shards(w):
        if chips != 4:
            every = lax.all_gather(w, "chip", axis=0, tiled=False)
            return [
                lax.dynamic_index_in_dim(every, chip ^ k, 0, keepdims=False)
                for k in range(1, chips)
            ]
        return [to_chip(w, 1), to_chip(w, 2)]

    def far_shard(near):
        if chips != 4:
            return []
        return [cat([to_chip(near[0][:1], 2), to_chip(near[1][1:], 1)], 0)]

    def both_cores(own):
        return [own, swap_core(own)]

    small = cat([norm_gain, norm_bias, qkv_bias.astype(f32).reshape(-1)])
    small = gather_axis(gather_axis(small, "core", 2), "chip", chips)
    small = small.reshape(2 * chips, -1)
    bias = small[:, 2 * n :].reshape(2 * chips, 3, -1)
    bias = bias.transpose(1, 0, 2).reshape(3, 1, width)
    vectors = gather_axis(small[:, : 2 * n], "tp", line)
    vectors = vectors.reshape(line, 2 * chips, 2, n).transpose(2, 1, 0, 3).reshape(2, D)

    rows = layer_input.shape[0]
    span = rows // 2
    tables = rotary_tables(line)

    def along_line(a):
        return lax.all_gather(a, "tp", axis=0, tiled=True)

    def summed_line(a):
        return lax.psum_scatter(a, "tp", scatter_dimension=0, tiled=True)

    slot = along_line(layer_input)
    w_od = lax.all_gather(cat([out_weight, down_weight], 0), "chip", axis=0, tiled=False)
    shard = after(gate_up_weight, small)
    near = near_shards(shard)
    slot = after(slot, *near)
    qkv_shard = after(qkv_weight, vectors, *near)
    w_gu = both_cores(jnp.stack([shard, *near, *far_shard(near)]))
    near = near_shards(qkv_shard) + ([to_chip(qkv_shard, 3)] if chips == 4 else [])
    w_qkv = both_cores(jnp.stack([qkv_shard, *near]))
    normed, stats, x, qkv = [None] * 2, [None] * 2, [None] * 2, [None] * 2
    for t in range(2):
        *normed[t], stats[t], x[t] = norm(scalars, t, span, slot, vectors, feats)
    for t in range(2):
        qkv[t] = joined_heads(scalars, normed[t], w_qkv, bias, tables[t])
    gate, up, acts = [None] * 2, [None] * 2, [None] * 2
    attn, lse, branch = [None] * 2, [None] * 2, [None] * 2
    attn[0], lse[0] = attend(0, span, qkv)
    w_od = both_cores(after(w_od, attn[0]))
    gate[0], up[0], acts[0] = gate_up(scalars, normed[0], attn[0], w_gu)
    branch[0] = branch_sums(scalars, acts[0], w_od)
    qkv[1] = after(qkv[1], branch[0])
    attn[1], lse[1] = attend(1, span, qkv)
    gate[1], up[1], acts[1] = gate_up(scalars, normed[1], attn[1], w_gu)
    branch[1] = branch_sums(scalars, acts[1], w_od)
    seeds, seed_all, losses = [None] * 2, [None] * 2, [None] * 2
    result = None
    for t in range(2):
        total = summed_line(branch[t])
        result, seeds[t], low, loss = finish(
            scalars, t, total, layer_input, teacher, out_grad, result, feats
        )
        losses[t] = jnp.sum(loss)
        seed_all[t] = along_line(low)

    half = D // 2

    def seed_half(t, h):
        return seed_all[t][:, h * half : (h + 1) * half]

    def od_part(t, h, *hold):
        return dot_tn(after(acts[t], *hold), seed_half(t, h))

    def with_other(mine, theirs):
        return (mine + theirs.astype(f32)).astype(bf16)

    def scattered(a, axis):
        return lax.psum_scatter(a, "chip", scatter_dimension=axis, tiled=True).astype(f32)

    def rows_of(a, k):
        return lax.dynamic_slice_in_dim(a, (chip ^ k) * feats, feats, 0)

    def sent_rows(a, some):
        return [to_chip(rows_of(a, k), k) for k in some]

    def gu_part(t, h, hold):
        return dot_tn(normed[t][h], after(grad_gu[t], hold))

    grad_attn, grad_gu = [None] * 2, [None] * 2
    grad_attn[0], grad_gu[0] = grad_acts(scalars, seed_all[0], w_od, gate[0], up[0])
    kept = attend_back(0, span, qkv, grad_attn[0], lse[0], tables)
    od_early = [od_part(0, h, kept[0]) for h in range(2)]
    gu_early = [gu_part(0, h, kept[0]) for h in range(2)]

    seed_all[1] = after(seed_all[1], *od_early, *gu_early)
    od_sent = (od_early[1] + od_part(1, 1)).astype(bf16)
    od_theirs = swap_core(od_sent)
    seed_all[1] = after(seed_all[1], od_sent)
    grad_attn[1], grad_gu[1] = grad_acts(scalars, seed_all[1], w_od, gate[1], up[1])
    od_sum = with_other(od_early[0] + od_part(1, 0, grad_gu[1]), od_theirs)
    od_grad = scattered(od_sum, 1)
    gu_sent = (gu_early[1] + gu_part(1, 1, od_sum)).astype(bf16)
    gu_theirs = swap_core(gu_sent)
    grad_qkv, grad_bias = attend_back(
        1, span, qkv, after(grad_attn[1], gu_sent), lse[1], tables, kept
    )
    gu_sum = with_other(gu_early[0] + gu_part(1, 0, grad_qkv), gu_theirs)
    normed_all = [cat([normed[0][h], normed[1][h]], 0) for h in range(2)]
    grads, gains, shifts, sums = [None] * 2, [None] * 2, [None] * 2, [None] * 2

    def back(t, hold):
        grads[t], gain, shift = grad_normed(
            scalars, t, after(grad_qkv, hold), grad_gu[t], w_qkv, w_gu, x[t], stats[t]
        )
        gains[t], shifts[t] = jnp.sum(gain, 0), jnp.sum(shift, 0)
        sums[t] = summed_line(grads[t])

    back(0, gu_sum)
    gu_got = sent_rows(gu_sum, (1, 2))
    qkv_held = after(grad_qkv, grads[0], *gu_got)
    qkv_sent = dot_tn(normed_all[1], qkv_held).astype(bf16)
    qkv_theirs = swap_core(qkv_sent)
    gu_got += sent_rows(after(gu_sum, *gu_got), range(3, chips))
    back(1, qkv_sent)
    qkv_held = after(qkv_held, grads[1], *gu_got)
    qkv_sum = with_other(dot_tn(normed_all[0], qkv_held), qkv_theirs)
    qkv_got = sent_rows(qkv_sum, range(1, chips))
    gu_grad = rows_of(gu_sum, 0).astype(f32) + sum(g.astype(f32) for g in gu_got)
    qkv_grad = rows_of(qkv_sum, 0).astype(f32) + sum(g.astype(f32) for g in qkv_got)
    input_grad = None
    for t in range(2):
        input_grad = last(
            scalars, t, sums[t], layer_input, vectors, seeds[t], input_grad, feats
        )
    gains = [(gains[0] + gains[1])[h * half : (h + 1) * half] for h in range(2)]
    shifts = [(shifts[0] + shifts[1])[h * half : (h + 1) * half] for h in range(2)]

    count = jnp.clip(lengths[0] - place * rows, 0, rows)
    scalar_sums = jnp.stack([losses[0] + losses[1], count.astype(f32)])
    scalar_sums = jnp.broadcast_to(scalar_sums, (chips, line, 2))
    heads = jnp.sum(grad_bias, 0).reshape(3, chips, 2, -1).transpose(2, 1, 0, 3)
    heads = [jnp.where(core == h, heads[0], heads[1]) for h in range(2)]
    small_sums = []
    for h in range(2):
        vector = jnp.stack([gains[h], shifts[h]]).reshape(2, chips, line, n)
        vector = cat([vector.transpose(1, 2, 0, 3).reshape(chips, line, 2 * n), scalar_sums], -1)
        small_sums.append(cat([vector.reshape(chips, -1), heads[h].reshape(chips, -1)], -1))
    small_sums = [after(v, qkv_grad) for v in small_sums]
    total = scatter_axis(small_sums[0] + swap_core(small_sums[1]), "chip", chips)
    cut = line * (2 * n + 2)
    qkv_b_grad = total[cut:].reshape(3, -1)
    total = scatter_axis(total[:cut].reshape(line, -1), "tp", line)
    gain_grad, bias_grad = total[:n], total[n : 2 * n]
    loss_value = total[2 * n] / (total[2 * n + 1] * D)
    return (
        result,
        loss_value,
        input_grad,
        gain_grad,
        bias_grad,
        jnp.stack([qkv_grad[:, j * width : (j + 1) * width] for j in range(3)]),
        qkv_b_grad,
        od_grad[:width],
        jnp.stack([gu_grad[:, j * hid : (j + 1) * hid] for j in range(2)]),
        od_grad[width:],
    )


def solution(mesh):
    chips, line = mesh.shape["fsdp"] // 2, mesh.shape["tp"]
    fine = Mesh(mesh.devices.reshape(chips, 2, line), ("chip", "core", "tp"))
    fsdp = ("chip", "core")
    tokens = P(fsdp + ("tp",), None)
    vector = P(fsdp + ("tp",))
    return jax.shard_map(
        functools.partial(per_device, chips, line),
        mesh=fine,
        in_specs=(
            tokens,
            tokens,
            tokens,
            P(fsdp),
            vector,
            vector,
            P(None, fsdp, "tp"),
            P(None, ("tp",) + fsdp),
            P("tp", fsdp),
            P(None, fsdp, "tp"),
            P("tp", fsdp),
        ),
        out_specs=(
            tokens,
            P(),
            tokens,
            vector,
            vector,
            P(None, fsdp, "tp"),
            P(None, ("tp",) + fsdp),
            P("tp", fsdp),
            P(None, fsdp, "tp"),
            P("tp", fsdp),
        ),
        check_vma=False,
    )
```

```python
import functools

import jax
import jax.numpy as jnp
from jax import lax
from jax.experimental import pallas as pl
from jax.experimental.pallas import tpu as pltpu
from jax.sharding import Mesh
from jax.sharding import PartitionSpec as P

D = 2048
HD = 64
ROT = 16
SEQ = 1024
PAIR = 2 * HD
SPAN = 256
epsilon = 1e-05
f32 = jnp.float32
bf16 = jnp.bfloat16


def after(value, *others):
    return lax.optimization_barrier((value,) + others)[0]


def swap_core(a):
    return lax.ppermute(a, "core", [(0, 1), (1, 0)])


def gather_axis(a, axis, n):
    me = lax.axis_index(axis)
    buf = a[None]
    k = 1
    while k < n:
        other = lax.ppermute(buf, axis, [(j, j ^ k) for j in range(n)])
        upper = (me // k) % 2 == 1
        buf = jnp.concatenate(
            [jnp.where(upper, other, buf), jnp.where(upper, buf, other)], 0
        )
        k *= 2
    return buf


def direct_sum(a, axis, n):
    me = lax.axis_index(axis)

    def row(k):
        return lax.dynamic_index_in_dim(a, me ^ k, 0, keepdims=False)

    sent = [lax.ppermute(row(k), axis, [(j, j ^ k) for j in range(n)]) for k in range(1, n)]
    return row(0) + sum(sent)


def rotary_tables(line):
    half_rot = ROT // 2
    positions = jnp.arange(SEQ, dtype=jnp.int32).astype(f32)
    frequency = 10000.0 ** (-2.0 * jnp.arange(half_rot, dtype=f32) / ROT)
    angles = positions[:, None] * frequency[None, :]
    cos, sin = jnp.cos(angles), jnp.sin(angles)
    rest = HD - ROT
    zero = jnp.zeros((SEQ, rest), f32)
    keep = jnp.concatenate([cos, cos, jnp.ones((SEQ, rest), f32)], -1)
    ahead = jnp.concatenate([-sin, jnp.zeros_like(sin), zero], -1)
    behind = jnp.concatenate([jnp.zeros_like(sin), sin, zero], -1)
    one = jnp.stack([keep, ahead, behind])
    one = jnp.concatenate([one, one], -1).reshape(3, line, 2, -1, PAIR)
    return [one[:, :, t].reshape(3, SEQ // 2, PAIR) for t in range(2)]


def turned(v, tab_ref, sign):
    half_rot = ROT // 2
    return (
        v * tab_ref[0]
        + sign
        * (
            pltpu.roll(v, PAIR - half_rot, 1) * tab_ref[1]
            + pltpu.roll(v, half_rot, 1) * tab_ref[2]
        )
    )


def dot_nt(a, b):
    return lax.dot_general(a, b, (((1,), (1,)), ((), ())), preferred_element_type=f32)


def dot_nn(a, b):
    return lax.dot_general(a, b, (((1,), (0,)), ((), ())), preferred_element_type=f32)


def dot_tn(a, b):
    return lax.dot_general(a, b, (((0,), (0,)), ((), ())), preferred_element_type=f32)


def two_heads(a):
    lane = lax.broadcasted_iota(jnp.int32, a.shape, 1)
    zero = jnp.zeros_like(a)
    return jnp.concatenate([jnp.where(lane < HD, a, zero), jnp.where(lane < HD, zero, a)], 0)


def one_row_each(a):
    rows = a.shape[1] // 2
    dim = lax.broadcasted_iota(jnp.int32, (PAIR, rows), 0)
    return jnp.where(dim < HD, a[:, :rows], a[:, rows:]).T


def spans(part, z, span):
    return ((z + 1) * span, (z + part) * span)


def masked(a, span, fill):
    lo = a.shape[0] - span
    key = lax.broadcasted_iota(jnp.int32, (span, 2 * span), 0)
    query = lax.broadcasted_iota(jnp.int32, (span, 2 * span), 1)
    query = jnp.where(query >= span, query - span, query)
    tail = jnp.where(key <= query, a[lo:], fill)
    return jnp.concatenate([a[:lo], tail], 0) if lo else tail


def attend_kernel(part, span, q_ref, k0_ref, v0_ref, k1_ref, v1_ref, attn_ref, lse_ref):
    keys, values = (k0_ref, k1_ref), (v0_ref[0].T, v1_ref[0].T)
    for z in range(SEQ // 2 // span):
        rows = slice(z * span, (z + 1) * span)
        q = two_heads(q_ref[0, rows, :])
        scores = {}
        for t, count in enumerate(spans(part, z, span)):
            if count:
                scores[t] = dot_nt(keys[t][0, :count, :], q)
        scores[part] = masked(scores[part], span, -1e30)
        top = functools.reduce(
            jnp.maximum, [jnp.max(a, 0, keepdims=True) for a in scores.values()]
        )
        scores = {t: jnp.exp(a - top) for t, a in scores.items()}
        total = sum(jnp.sum(a, 0, keepdims=True) for a in scores.values())
        inverse = 1.0 / total
        out = sum(
            dot_nn(values[t][:, : a.shape[0]], (a * inverse).astype(bf16))
            for t, a in scores.items()
        )
        attn_ref[rows, :] = one_row_each(out).astype(bf16)
        lse_ref[0, z : z + 1, :] = top + jnp.log(total)


def head_spec(j):
    return pl.BlockSpec((1, SEQ // 2, PAIR), lambda p: (j, 0, p))


def attend(part, span, qkv):
    width = qkv[0].shape[2]
    pairs = width // PAIR
    blocks = SEQ // 2 // span
    half = SEQ // 2
    mine = pl.BlockSpec((half, PAIR), lambda p: (0, p))
    return pl.pallas_call(
        functools.partial(attend_kernel, part, span),
        grid=(pairs,),
        in_specs=[head_spec(0), head_spec(1), head_spec(2), head_spec(1), head_spec(2)],
        out_specs=[mine, pl.BlockSpec((1, blocks, 2 * span), lambda p: (p, 0, 0))],
        out_shape=[
            jax.ShapeDtypeStruct((half, width), bf16),
            jax.ShapeDtypeStruct((pairs, blocks, 2 * span), f32),
        ],
        compiler_params=pltpu.CompilerParams(vmem_limit_bytes=(56 if part else 30) << 20),
        cost_estimate=pl.CostEstimate(
            flops=pairs * SEQ * SEQ * PAIR * 4,
            transcendentals=pairs * SEQ * SEQ,
            bytes_accessed=10 * SEQ * width,
        ),
        name="attend",
    )(qkv[part], qkv[0], qkv[0], qkv[1], qkv[1])


def attend_back_kernel(
    part, span, q_ref, k0_ref, v0_ref, k1_ref, v1_ref, grad_ref, lse_ref, tab0_ref, tab1_ref, *refs
):
    scale = HD ** (-0.5)
    half = SEQ // 2
    if part == 0:
        gq_ref, *gkv_refs = refs
        sums = gkv_refs
        for ref in sums:
            ref[...] = jnp.zeros_like(ref)
    else:
        gq0_ref, *kept = refs[:5]
        out_ref, bias_ref, gq_ref, *sums = refs[5:]
        for ref, old in zip(sums, kept):
            ref[...] = old[...]
    keys, values = (k0_ref, k1_ref), (v0_ref, v1_ref)
    turned_keys = (k0_ref[0].T, k1_ref[0].T)
    for z in range(half // span):
        rows = slice(z * span, (z + 1) * span)
        q, g = two_heads(q_ref[0, rows, :]), two_heads(grad_ref[rows, :])
        lse = lse_ref[0, z : z + 1, :]
        probs, gprobs = {}, {}
        inner = 0.0
        for t, count in enumerate(spans(part, z, span)):
            if count:
                p = jnp.exp(dot_nt(keys[t][0, :count, :], q) - lse)
                probs[t] = masked(p, span, 0.0) if t == part else p
                gprobs[t] = dot_nt(values[t][0, :count, :], g)
                inner = inner + jnp.sum(probs[t] * gprobs[t], 0, keepdims=True)
        gq = 0.0
        for t, p in probs.items():
            count = p.shape[0]
            gs = (p * (gprobs[t] - inner)).astype(bf16)
            sums[2 * t][:count, :] += dot_nn(gs, q)
            sums[2 * t + 1][:count, :] += dot_nn(p.astype(bf16), g)
            gq = gq + dot_nn(turned_keys[t][:, :count], gs)
        gq_ref[rows, :] = one_row_each(gq) * scale
    if part == 1:
        pairs = pl.num_programs(0)
        pair = pl.program_id(0)
        for j in range(3):
            lanes = pl.ds(pl.multiple_of((j * pairs + pair) * PAIR, PAIR), PAIR)
            bias = 0.0
            for t, tab_ref in enumerate((tab0_ref, tab1_ref)):
                g = sums[2 * t + j - 1][...] if j else (gq_ref if t else gq0_ref)[...]
                if j < 2:
                    g = turned(g, tab_ref, -1.0)
                g = g.astype(bf16)
                out_ref[t * half : (t + 1) * half, lanes] = g
                bias = bias + jnp.sum(g.astype(f32).reshape(half // 8, 8, PAIR), 0)
            bias_ref[:, lanes] = bias


def attend_back(part, span, qkv, grad, lse, tables, kept=()):
    width = grad.shape[1]
    pairs = width // PAIR
    blocks = SEQ // 2 // span
    half = SEQ // 2
    mine = pl.BlockSpec((half, PAIR), lambda p: (0, p))
    table = pl.BlockSpec((3, half, PAIR), lambda p: (0, 0, 0))
    partial_shapes = [jax.ShapeDtypeStruct((half, width), f32)] * 5
    if part == 0:
        out_specs, out_shape, scratch = [mine] * 5, partial_shapes, []
    else:
        out_specs = [
            pl.BlockSpec((SEQ, 3 * width), lambda p: (0, 0)),
            pl.BlockSpec((8, 3 * width), lambda p: (0, 0)),
        ]
        out_shape = [
            jax.ShapeDtypeStruct((SEQ, 3 * width), bf16),
            jax.ShapeDtypeStruct((8, 3 * width), f32),
        ]
        scratch = [pltpu.VMEM((half, PAIR), f32)] * 5
    return pl.pallas_call(
        functools.partial(attend_back_kernel, part, span),
        grid=(pairs,),
        in_specs=[head_spec(0), head_spec(1), head_spec(2), head_spec(1), head_spec(2)]
        + [mine, pl.BlockSpec((1, blocks, 2 * span), lambda p: (p, 0, 0)), table, table]
        + [mine] * len(kept),
        out_specs=out_specs,
        out_shape=out_shape,
        scratch_shapes=scratch,
        compiler_params=pltpu.CompilerParams(vmem_limit_bytes=(56 if part else 30) << 20),
        cost_estimate=pl.CostEstimate(
            flops=pairs * SEQ * SEQ * PAIR * 10,
            transcendentals=pairs * SEQ * SEQ,
            bytes_accessed=20 * SEQ * width,
        ),
        name="attend_back",
    )(qkv[part], qkv[0], qkv[0], qkv[1], qkv[1], grad, lse, *tables, *kept)


def call(kernel, name, grid, in_specs, out_specs, out_shape, scalars, args, flops=0, scratch=(), vmem=30):
    moved = sum(a.size * a.dtype.itemsize for a in args)
    moved += sum(o.size * jnp.dtype(o.dtype).itemsize for o in out_shape)
    return pl.pallas_call(
        kernel,
        grid_spec=pltpu.PrefetchScalarGridSpec(
            num_scalar_prefetch=1,
            grid=grid,
            in_specs=in_specs,
            out_specs=out_specs,
            scratch_shapes=scratch,
        ),
        out_shape=out_shape,
        compiler_params=pltpu.CompilerParams(vmem_limit_bytes=vmem << 20),
        cost_estimate=pl.CostEstimate(flops=flops, transcendentals=0, bytes_accessed=moved),
        name=name,
    )(scalars, *args)


def whole_spec(shape):
    zeros = (0,) * len(shape)
    return pl.BlockSpec(shape, lambda i, s: zeros, pipeline_mode=pl.Buffered(1))


def shard_spec(w):
    rest = (0,) * (w.ndim - 1)
    return pl.BlockSpec((1,) + w.shape[1:], lambda k, s: (k,) + rest)


def all_spec(rows, cols):
    return pl.BlockSpec((rows, cols), lambda k, s: (0, 0), pipeline_mode=pl.Buffered(1))


def over_rows(rows, step, body):
    @pl.loop(0, rows // step)
    def _(i):
        body(pl.ds(pl.multiple_of(i * step, step), step))


def row_spec(rows, cols):
    return pl.BlockSpec((rows, cols), lambda i, s: (i, 0))


def shape_of(shape, dtype):
    return jax.ShapeDtypeStruct(shape, dtype)


def lanes_of(scalar_ref, h, p, feats):
    block = 2 * p + jnp.bitwise_xor(scalar_ref[0], h)
    return pl.ds(pl.multiple_of(block * feats, feats), feats)


def shard_lanes(scalar_ref, k, feats, first=0):
    block = jnp.bitwise_xor(scalar_ref[1], k)
    return pl.ds(pl.multiple_of(first + block * feats, feats), feats)


def moments(x):
    mean = jnp.sum(x, -1, keepdims=True) / D
    x = x - mean
    return mean, lax.rsqrt(jnp.sum(x * x, -1, keepdims=True) / D + epsilon)


def norm_kernel(feats, s_ref, x_ref, vec_ref, own_ref, other_ref, stat_ref, copy_ref):
    mean, inv = moments(x_ref[...].astype(f32))
    copy_ref[...] = x_ref[...]
    for h, out_ref in enumerate((own_ref, other_ref)):
        for p in range(D // (2 * feats)):
            at = lanes_of(s_ref, h, p, feats)
            u = (x_ref[:, at].astype(f32) - mean) * inv
            out_ref[:, p * feats : (p + 1) * feats] = (
                u * vec_ref[0:1, at] + vec_ref[1:2, at]
            ).astype(bf16)
    lane = lax.broadcasted_iota(jnp.int32, stat_ref.shape, 1)
    stat_ref[...] = jnp.where(lane < PAIR // 2, mean, inv)


def norm(scalars, part, span, x, vectors, feats):
    half = D // 2
    rows = SEQ // 2
    return call(
        functools.partial(norm_kernel, feats),
        "norm",
        (rows // span,),
        [pl.BlockSpec((span, D), lambda z, s: (2 * z + part, 0)), whole_spec((2, D))],
        [row_spec(span, half), row_spec(span, half), row_spec(span, PAIR), row_spec(span, D)],
        [shape_of((rows, half), bf16)] * 2
        + [shape_of((rows, PAIR), f32), shape_of((rows, D), bf16)],
        scalars,
        (x, vectors),
    )


def joined_kernel(
    s_ref, own_ref, other_ref, bias_ref, tab_ref, w0_ref, w1_ref, out_ref, sum_ref
):
    _, many, feats, width = w0_ref.shape
    k, last_k = pl.program_id(0), pl.num_programs(0) - 1
    at = shard_lanes(s_ref, k, feats)
    rows = own_ref.shape[0]

    @pl.when(k == 0)
    def _():
        for j in range(many):
            sum_ref[j] = jnp.broadcast_to(bias_ref[j], (rows, width))

    def step(here):
        x0, x1 = own_ref[here, at], other_ref[here, at]
        for j in range(many):
            sum_ref[j, here, :] += dot_nn(x0, w0_ref[0, j]) + dot_nn(x1, w1_ref[0, j])

    over_rows(rows, SPAN, step)

    @pl.when(k == last_k)
    def _():
        def rotate(here):
            tab = tab_ref[:, here, :]
            for j in range(2):
                scale = 1.0 if j else HD ** (-0.5)
                for p in range(width // PAIR):
                    lanes = slice(p * PAIR, (p + 1) * PAIR)
                    out_ref[j, here, lanes] = (
                        turned(sum_ref[j, here, lanes], tab, 1.0) * scale
                    ).astype(bf16)
            out_ref[2, here, :] = sum_ref[2, here, :].astype(bf16)

        over_rows(rows, 64, rotate)


def joined_heads(scalars, normed, weights, bias, table):
    chips, many, _, width = weights[0].shape
    rows = normed[0].shape[0]
    return call(
        joined_kernel,
        "joined",
        (chips,),
        [all_spec(rows, D // 2)] * 2
        + [whole_spec((3, 1, width)), whole_spec((3, rows, PAIR))]
        + [shard_spec(w) for w in weights],
        [pl.BlockSpec((3, rows, width), lambda k, s: (0, 0, 0))],
        [shape_of((3, rows, width), bf16)],
        scalars,
        (*normed, bias, table, *weights),
        flops=2 * rows * D * 3 * width,
        scratch=[pltpu.VMEM((many, rows, width), f32)],
    )[0]


def gate_up_kernel(
    s_ref, own_ref, other_ref, attn_ref, w0_ref, w1_ref, gate_ref, up_ref, acts_ref
):
    width = attn_ref.shape[1]
    feats = w0_ref.shape[2]
    k, last_k = pl.program_id(0), pl.num_programs(0) - 1
    at = shard_lanes(s_ref, k, feats)
    rows = own_ref.shape[0]

    @pl.when(k == 0)
    def _():
        gate_ref[...] = jnp.zeros_like(gate_ref)
        up_ref[...] = jnp.zeros_like(up_ref)
        acts_ref[:, :width] = attn_ref[...]

    def step(here):
        x0, x1 = own_ref[here, at], other_ref[here, at]
        for j, out_ref in enumerate((gate_ref, up_ref)):
            out_ref[here, :] += dot_nn(x0, w0_ref[0, j]) + dot_nn(x1, w1_ref[0, j])

    over_rows(rows, SPAN, step)

    @pl.when(k == last_k)
    def _():
        def join(here):
            gate = gate_ref[here, :]
            acts_ref[here, width:] = (gate * jax.nn.sigmoid(gate) * up_ref[here, :]).astype(bf16)

        over_rows(rows, 64, join)


def gate_up(scalars, normed, attn, weights):
    chips, _, _, hid = weights[0].shape
    rows, width = attn.shape
    return call(
        gate_up_kernel,
        "gate_up",
        (chips,),
        [all_spec(rows, D // 2)] * 2
        + [all_spec(rows, width)]
        + [shard_spec(w) for w in weights],
        [all_spec(rows, hid), all_spec(rows, hid), all_spec(rows, width + hid)],
        [shape_of((rows, hid), f32)] * 2 + [shape_of((rows, width + hid), bf16)],
        scalars,
        (*normed, attn, *weights),
        flops=4 * rows * D * hid,
    )


def branch_kernel(s_ref, acts_ref, w0_ref, w1_ref, out_ref):
    feats = w0_ref.shape[2]
    p = pl.program_id(0)
    rows = acts_ref.shape[0]

    def step(here):
        acts = acts_ref[here, :]
        for h, w_ref in enumerate((w0_ref, w1_ref)):
            at = pl.ds(pl.multiple_of(h * D // 2 + p * feats, feats), feats)
            out_ref[here, at] = dot_nn(acts, w_ref[0]).astype(bf16)

    over_rows(rows, SPAN, step)


def branch_sums(scalars, acts, weights):
    chips = weights[0].shape[0]
    rows, deep = acts.shape
    return call(
        branch_kernel,
        "branch",
        (chips,),
        [all_spec(rows, deep)] + [shard_spec(w) for w in weights],
        [all_spec(rows, D)],
        [shape_of((rows, D), bf16)],
        scalars,
        (acts, *weights),
        flops=2 * rows * deep * D,
    )[0]


def finish_kernel(
    feats, part, s_ref, branch_ref, x_ref, teach_ref, cot_ref, old_ref,
    result_ref, seed_ref, low_ref, loss_ref,
):
    rows = x_ref.shape[0]
    first = (2 * s_ref[2] + part) * rows
    valid = (first + lax.broadcasted_iota(jnp.int32, (rows, 1), 0) < s_ref[3]).astype(f32)
    loss = jnp.zeros((8, PAIR), f32)
    chips = D // (2 * feats)
    for h in range(2):
        for k in range(chips):
            at = lanes_of(s_ref, h, k, feats)
            here = slice((h * chips + k) * feats, (h * chips + k + 1) * feats)
            y = x_ref[:, at].astype(f32) + valid * branch_ref[:, here].astype(f32)
            mismatch = y - teach_ref[:, at].astype(f32)
            square = jnp.sum((valid * mismatch * mismatch).reshape(rows // 8, 8, feats), 0)
            for q in range(feats // PAIR):
                loss = loss + square[:, q * PAIR : (q + 1) * PAIR]
            seed = valid * (cot_ref[:, at].astype(f32) + mismatch)
            result_ref[:, at] = y.astype(bf16)
            seed_ref[:, at] = seed
            low_ref[:, here] = seed.astype(bf16)
    loss_ref[...] = loss


def part_spec(rows, cols, part):
    return pl.BlockSpec((rows, cols), lambda i, s: (part, 0))


def aliased(kernel, name, in_specs, out_specs, out_shape, scalars, args, aliases):
    moved = sum(o.size * jnp.dtype(o.dtype).itemsize for o in out_shape)
    return pl.pallas_call(
        kernel,
        grid_spec=pltpu.PrefetchScalarGridSpec(
            num_scalar_prefetch=1, grid=(1,), in_specs=in_specs, out_specs=out_specs
        ),
        out_shape=out_shape,
        input_output_aliases=aliases,
        compiler_params=pltpu.CompilerParams(vmem_limit_bytes=24 << 20),
        cost_estimate=pl.CostEstimate(flops=0, transcendentals=0, bytes_accessed=3 * moved),
        name=name,
    )(scalars, *args)


def finish(scalars, part, branch, x, teacher, out_grad, old, feats):
    rows = branch.shape[0]
    mine = part_spec(rows, D, part)
    one = part_spec(rows, D, 0)
    aliases = {}
    if old is None:
        old = jnp.zeros((8, PAIR), bf16)
        old_spec = part_spec(8, PAIR, 0)
    else:
        old_spec = pl.BlockSpec(memory_space=pl.ANY)
        aliases = {5: 0}
    return aliased(
        functools.partial(finish_kernel, feats, part),
        "finish",
        [one, mine, mine, mine, old_spec],
        [mine, one, one, part_spec(8, PAIR, 0)],
        [
            shape_of((2 * rows, D), bf16),
            shape_of((rows, D), f32),
            shape_of((rows, D), bf16),
            shape_of((8, PAIR), f32),
        ],
        scalars,
        (branch, x, teacher, out_grad, old),
        aliases,
    )


def grad_acts_kernel(
    s_ref, seed_ref, gate_ref, up_ref, w0_ref, w1_ref, attn_ref, gu_ref, sum_ref
):
    hid = gate_ref.shape[1]
    width = attn_ref.shape[1]
    feats = w0_ref.shape[2]
    p, last_p = pl.program_id(0), pl.num_programs(0) - 1
    rows = seed_ref.shape[0]

    @pl.when(p == 0)
    def _():
        sum_ref[...] = jnp.zeros_like(sum_ref)

    def step(here):
        total = sum_ref[here, :]
        for h, w_ref in enumerate((w0_ref, w1_ref)):
            at = pl.ds(pl.multiple_of(h * D // 2 + p * feats, feats), feats)
            total = total + dot_nt(seed_ref[here, at], w_ref[0])
        sum_ref[here, :] = total

    over_rows(rows, SPAN, step)

    @pl.when(p == last_p)
    def _():
        def split(here):
            attn_ref[here, :] = sum_ref[here, :width].astype(bf16)
            grad = sum_ref[here, width:]
            gate, up = gate_ref[here, :], up_ref[here, :]
            sigmoid = jax.nn.sigmoid(gate)
            gu_ref[here, :hid] = (
                grad * up * sigmoid * (1.0 + gate * (1.0 - sigmoid))
            ).astype(bf16)
            gu_ref[here, hid:] = (grad * gate * sigmoid).astype(bf16)

        over_rows(rows, 64, split)


def grad_acts(scalars, seed, weights, gate, up):
    chips, deep, _ = weights[0].shape
    rows, hid = gate.shape
    width = deep - hid
    return call(
        grad_acts_kernel,
        "grad_acts",
        (chips,),
        [all_spec(rows, D), all_spec(rows, hid), all_spec(rows, hid)]
        + [shard_spec(w) for w in weights],
        [all_spec(rows, width), all_spec(rows, 2 * hid)],
        [shape_of((rows, width), bf16), shape_of((rows, 2 * hid), bf16)],
        scalars,
        (seed, gate, up, *weights),
        flops=2 * rows * D * deep,
        scratch=[pltpu.VMEM((rows, deep), f32)],
    )


def grad_normed_kernel(s_ref, qkv_ref, gu_ref, x_ref, stat_ref, *refs):
    w_refs, (out_ref, gain_ref, shift_ref) = refs[:4], refs[4:]
    feats = w_refs[0].shape[2]
    k = pl.program_id(0)
    rows = x_ref.shape[0]
    at = [shard_lanes(s_ref, k, feats, h * D // 2) for h in range(2)]
    for h in range(2):
        gain_ref[:, at[h]] = jnp.zeros((8, feats), f32)
        shift_ref[:, at[h]] = jnp.zeros((8, feats), f32)

    def step(here):
        mean, inv = stat_ref[here, 0:1], stat_ref[here, PAIR // 2 : PAIR // 2 + 1]
        for h in range(2):
            g = 0.0
            for a_ref, w_ref in ((qkv_ref, w_refs[h]), (gu_ref, w_refs[2 + h])):
                _, many, _, wide = w_ref.shape
                for j in range(many):
                    g = g + dot_nt(a_ref[here, j * wide : (j + 1) * wide], w_ref[0, j])
            out_ref[here, at[h]] = g.astype(bf16)
            lanes = lanes_of(s_ref, h, jnp.bitwise_xor(s_ref[1], k), feats)
            u = (x_ref[here, lanes].astype(f32) - mean) * inv
            gain_ref[:, at[h]] += jnp.sum((g * u).reshape(-1, 8, feats), 0)
            shift_ref[:, at[h]] += jnp.sum(g.reshape(-1, 8, feats), 0)

    over_rows(rows, SPAN, step)


def grad_normed(scalars, part, grad_qkv, grad_gu, w_qkv, w_gu, x, stats):
    chips, _, _, width = w_qkv[0].shape
    hid = w_gu[0].shape[3]
    rows = x.shape[0]
    weights = (*w_qkv, *w_gu)
    return call(
        grad_normed_kernel,
        "grad_normed",
        (chips,),
        [
            pl.BlockSpec((rows, 3 * width), lambda k, s: (part, 0)),
            all_spec(rows, 2 * hid),
            all_spec(rows, D),
            all_spec(rows, PAIR),
        ]
        + [shard_spec(w) for w in weights],
        [all_spec(rows, D), all_spec(8, D), all_spec(8, D)],
        [shape_of((rows, D), bf16), shape_of((8, D), f32), shape_of((8, D), f32)],
        scalars,
        (grad_qkv, grad_gu, x, stats, *weights),
        flops=2 * rows * D * (3 * width + 2 * hid),
        vmem=56 if part else 30,
    )


def last_kernel(feats, s_ref, sum_ref, x_ref, vec_ref, seed_ref, old_ref, out_ref):
    mean, inv = moments(x_ref[...].astype(f32))
    chips = D // (2 * feats)

    def units(h, k):
        here = slice((h * chips + k) * feats, (h * chips + k + 1) * feats)
        at = lanes_of(s_ref, h, k, feats)
        g = sum_ref[:, here].astype(f32) * vec_ref[0:1, at]
        return g, (x_ref[:, at].astype(f32) - mean) * inv, at

    m1 = m2 = 0.0
    for h in range(2):
        for k in range(chips):
            g, u, _ = units(h, k)
            m1 = m1 + jnp.sum(g, -1, keepdims=True)
            m2 = m2 + jnp.sum(g * u, -1, keepdims=True)
    m1, m2 = m1 / D, m2 / D
    for h in range(2):
        for k in range(chips):
            g, u, at = units(h, k)
            out_ref[:, at] = (seed_ref[:, at] + inv * (g - m1 - u * m2)).astype(bf16)


def last(scalars, part, total, x, vectors, seed, old, feats):
    rows = total.shape[0]
    mine = part_spec(rows, D, part)
    one = part_spec(rows, D, 0)
    aliases = {}
    if old is None:
        old = jnp.zeros((8, PAIR), bf16)
        old_spec = part_spec(8, PAIR, 0)
    else:
        old_spec = pl.BlockSpec(memory_space=pl.ANY)
        aliases = {5: 0}
    return aliased(
        functools.partial(last_kernel, feats),
        "last",
        [one, mine, part_spec(2, D, 0), one, old_spec],
        [mine],
        [shape_of((2 * rows, D), bf16)],
        scalars,
        (total, x, vectors, seed, old),
        aliases,
    )[0]


def per_device(
    chips,
    line,
    layer_input,
    teacher,
    out_grad,
    lengths,
    norm_gain,
    norm_bias,
    qkv_weight,
    qkv_bias,
    out_weight,
    gate_up_weight,
    down_weight,
):
    core = lax.axis_index("core")
    chip = lax.axis_index("chip")
    place = lax.axis_index("tp")
    scalars = jnp.stack([core, chip, place, lengths[0]]).astype(jnp.int32)
    feats = D // (2 * chips)
    width = qkv_weight.shape[2]
    hid = down_weight.shape[0]
    n = norm_gain.shape[0]
    cat = jnp.concatenate

    def to_chip(a, k):
        return lax.ppermute(a, "chip", [(c, c ^ k) for c in range(chips)])

    def near_shards(w):
        if chips != 4:
            every = lax.all_gather(w, "chip", axis=0, tiled=False)
            return [
                lax.dynamic_index_in_dim(every, chip ^ k, 0, keepdims=False)
                for k in range(1, chips)
            ]
        return [to_chip(w, 1), to_chip(w, 2)]

    def far_shard(near):
        if chips != 4:
            return []
        cut = feats // 2
        return [cat([to_chip(near[0][:, :cut], 2), to_chip(near[1][:, cut:], 1)], 1)]

    def both_cores(own):
        return [own, swap_core(own)]

    small = cat([norm_gain, norm_bias, qkv_bias.astype(f32).reshape(-1)])
    small = gather_axis(gather_axis(small, "core", 2), "chip", chips)
    small = small.reshape(2 * chips, -1)
    bias = small[:, 2 * n :].reshape(2 * chips, 3, -1)
    bias = bias.transpose(1, 0, 2).reshape(3, 1, width)
    vectors = gather_axis(small[:, : 2 * n], "tp", line)
    vectors = vectors.reshape(line, 2 * chips, 2, n).transpose(2, 1, 0, 3).reshape(2, D)

    rows = layer_input.shape[0]
    span = rows // 2
    tables = rotary_tables(line)

    def along_line(a):
        return lax.all_gather(a, "tp", axis=0, tiled=True)

    def summed_line(a):
        return lax.psum_scatter(a, "tp", scatter_dimension=0, tiled=True)

    slot = along_line(layer_input)
    w_od = lax.all_gather(cat([out_weight, down_weight], 0), "chip", axis=0, tiled=False)
    shard = after(gate_up_weight, small)
    near = near_shards(shard)
    slot = after(slot, *near)
    qkv_shard = after(qkv_weight, vectors, *tables, *near)
    w_gu = both_cores(jnp.stack([shard, *near, *far_shard(near)]))
    near = near_shards(qkv_shard)
    w_qkv = both_cores(jnp.stack([qkv_shard, *near, *far_shard(near)]))
    normed, stats, x, qkv = [None] * 2, [None] * 2, [None] * 2, [None] * 2
    for t in range(2):
        *normed[t], stats[t], x[t] = norm(scalars, t, span, slot, vectors, feats)
    for t in range(2):
        qkv[t] = joined_heads(scalars, normed[t], w_qkv, bias, tables[t])
    gate, up, acts = [None] * 2, [None] * 2, [None] * 2
    attn, lse, branch = [None] * 2, [None] * 2, [None] * 2
    attn[0], lse[0] = attend(0, span, qkv)
    w_od = both_cores(after(w_od, attn[0]))
    gate[0], up[0], acts[0] = gate_up(scalars, normed[0], attn[0], w_gu)
    branch[0] = branch_sums(scalars, acts[0], w_od)
    qkv[1] = after(qkv[1], branch[0])
    attn[1], lse[1] = attend(1, span, qkv)
    gate[1], up[1], acts[1] = gate_up(scalars, normed[1], attn[1], w_gu)
    branch[1] = branch_sums(scalars, acts[1], w_od)
    seeds, seed_all, losses = [None] * 2, [None] * 2, [None] * 2
    result = None
    for t in range(2):
        total = summed_line(branch[t])
        result, seeds[t], low, loss = finish(
            scalars, t, total, layer_input, teacher, out_grad, result, feats
        )
        losses[t] = jnp.sum(loss)
        seed_all[t] = along_line(low)

    half = D // 2

    def with_other(mine, theirs):
        return (mine + theirs.astype(f32)).astype(bf16)

    def scattered(a, axis):
        return lax.psum_scatter(a, "chip", scatter_dimension=axis, tiled=True).astype(f32)

    def rows_of(a, k):
        return lax.dynamic_slice_in_dim(a, (chip ^ k) * feats, feats, 0)

    def sent_rows(a, some):
        return [to_chip(rows_of(a, k), k) for k in some]

    acts_all = cat(acts, 0)
    normed_all = [cat([normed[0][h], normed[1][h]], 0) for h in range(2)]
    grad_attn, grad_gu = [None] * 2, [None] * 2
    grad_attn[0], grad_gu[0] = grad_acts(scalars, seed_all[0], w_od, gate[0], up[0])
    kept = attend_back(0, span, qkv, grad_attn[0], lse[0], tables)

    seed_all[1] = after(seed_all[1], kept[0], acts_all, *normed_all)
    seeds_all = cat(seed_all, 0)
    od_sent = dot_tn(acts_all, seeds_all[:, half:]).astype(bf16)
    od_theirs = swap_core(od_sent)
    seed_all[1] = after(seed_all[1], od_sent)
    grad_attn[1], grad_gu[1] = grad_acts(scalars, seed_all[1], w_od, gate[1], up[1])
    od_sum = dot_tn(acts_all, after(seeds_all, grad_gu[1])[:, :half])
    od_sum = with_other(od_sum, od_theirs)
    od_grad = scattered(od_sum, 1)
    gu_all = cat([grad_gu[0], after(grad_gu[1], od_sum)], 0)
    gu_sent = dot_tn(normed_all[1], gu_all).astype(bf16)
    gu_theirs = swap_core(gu_sent)
    grad_qkv, grad_bias = attend_back(
        1, span, qkv, after(grad_attn[1], gu_sent), lse[1], tables, kept
    )
    gu_sum = with_other(dot_tn(normed_all[0], after(gu_all, grad_qkv)), gu_theirs)
    grads, gains, shifts, sums = [None] * 2, [None] * 2, [None] * 2, [None] * 2

    def back(t, *hold):
        grads[t], gain, shift = grad_normed(
            scalars, t, after(grad_qkv, *hold), grad_gu[t], w_qkv, w_gu, x[t], stats[t]
        )
        gains[t], shifts[t] = jnp.sum(gain, 0), jnp.sum(shift, 0)
        sums[t] = summed_line(grads[t])

    qkv_held = after(grad_qkv, gu_sum)
    qkv_sent = dot_tn(normed_all[1], qkv_held).astype(bf16)
    qkv_theirs = swap_core(qkv_sent)
    gu_got = sent_rows(gu_sum, (1, 2))
    back(0, qkv_sent)
    qkv_back = after(grad_qkv, grads[0], *gu_got)
    gu_got += sent_rows(after(gu_sum, qkv_back), range(3, chips))
    back(1, qkv_back)
    qkv_held = after(qkv_held, grads[1], *gu_got)
    qkv_sum = with_other(dot_tn(normed_all[0], qkv_held), qkv_theirs)
    input_grad = None
    for t in range(2):
        input_grad = last(
            scalars, t, sums[t], layer_input, vectors, seeds[t], input_grad, feats
        )
    gains = [(gains[0] + gains[1])[h * half : (h + 1) * half] for h in range(2)]
    shifts = [(shifts[0] + shifts[1])[h * half : (h + 1) * half] for h in range(2)]

    count = jnp.clip(lengths[0] - place * rows, 0, rows)
    scalar_sums = jnp.stack([losses[0] + losses[1], count.astype(f32)])
    scalar_sums = jnp.broadcast_to(scalar_sums, (chips, line, 2))
    heads = jnp.sum(grad_bias, 0).reshape(3, chips, 2, -1).transpose(2, 1, 0, 3)
    heads = [jnp.where(core == h, heads[0], heads[1]) for h in range(2)]
    small_sums = []
    for h in range(2):
        vector = jnp.stack([gains[h], shifts[h]]).reshape(2, chips, line, n)
        vector = cat([vector.transpose(1, 2, 0, 3).reshape(chips, line, 2 * n), scalar_sums], -1)
        small_sums.append(cat([vector.reshape(chips, -1), heads[h].reshape(chips, -1)], -1))
    small_sums = [after(v, *gu_got) for v in small_sums]
    total = direct_sum(small_sums[0] + swap_core(small_sums[1]), "chip", chips)
    qkv_got = sent_rows(after(qkv_sum, total), range(1, chips))
    gu_grad = rows_of(gu_sum, 0).astype(f32) + sum(g.astype(f32) for g in gu_got)
    qkv_grad = rows_of(qkv_sum, 0).astype(f32) + sum(g.astype(f32) for g in qkv_got)
    cut = line * (2 * n + 2)
    qkv_b_grad = total[cut:].reshape(3, -1)
    total = direct_sum(total[:cut].reshape(line, -1), "tp", line)
    gain_grad, bias_grad = total[:n], total[n : 2 * n]
    loss_value = total[2 * n] / (total[2 * n + 1] * D)
    return (
        result,
        loss_value,
        input_grad,
        gain_grad,
        bias_grad,
        jnp.stack([qkv_grad[:, j * width : (j + 1) * width] for j in range(3)]),
        qkv_b_grad,
        od_grad[:width],
        jnp.stack([gu_grad[:, j * hid : (j + 1) * hid] for j in range(2)]),
        od_grad[width:],
    )


def solution(mesh):
    chips, line = mesh.shape["fsdp"] // 2, mesh.shape["tp"]
    fine = Mesh(mesh.devices.reshape(chips, 2, line), ("chip", "core", "tp"))
    fsdp = ("chip", "core")
    tokens = P(fsdp + ("tp",), None)
    vector = P(fsdp + ("tp",))
    return jax.shard_map(
        functools.partial(per_device, chips, line),
        mesh=fine,
        in_specs=(
            tokens,
            tokens,
            tokens,
            P(fsdp),
            vector,
            vector,
            P(None, fsdp, "tp"),
            P(None, ("tp",) + fsdp),
            P("tp", fsdp),
            P(None, fsdp, "tp"),
            P("tp", fsdp),
        ),
        out_specs=(
            tokens,
            P(),
            tokens,
            vector,
            vector,
            P(None, fsdp, "tp"),
            P(None, ("tp",) + fsdp),
            P("tp", fsdp),
            P(None, fsdp, "tp"),
            P("tp", fsdp),
        ),
        check_vma=False,
    )
```

```python
import functools

import jax
import jax.numpy as jnp
from jax import lax
from jax.experimental import pallas as pl
from jax.experimental.pallas import tpu as pltpu
from jax.sharding import Mesh
from jax.sharding import PartitionSpec as P

D = 2048
HD = 64
ROT = 16
SEQ = 1024
PAIR = 2 * HD
SPAN = 256
epsilon = 1e-05
f32 = jnp.float32
bf16 = jnp.bfloat16


def after(value, *others):
    return lax.optimization_barrier((value,) + others)[0]


def swap_core(a):
    return lax.ppermute(a, "core", [(0, 1), (1, 0)])


def gather_axis(a, axis, n):
    me = lax.axis_index(axis)
    buf = a[None]
    k = 1
    while k < n:
        other = lax.ppermute(buf, axis, [(j, j ^ k) for j in range(n)])
        upper = (me // k) % 2 == 1
        buf = jnp.concatenate(
            [jnp.where(upper, other, buf), jnp.where(upper, buf, other)], 0
        )
        k *= 2
    return buf


def direct_sum(a, axis, n):
    me = lax.axis_index(axis)

    def row(k):
        return lax.dynamic_index_in_dim(a, me ^ k, 0, keepdims=False)

    sent = [lax.ppermute(row(k), axis, [(j, j ^ k) for j in range(n)]) for k in range(1, n)]
    return row(0) + sum(sent)


def rotary_tables(line):
    half_rot = ROT // 2
    positions = jnp.arange(SEQ, dtype=jnp.int32).astype(f32)
    frequency = 10000.0 ** (-2.0 * jnp.arange(half_rot, dtype=f32) / ROT)
    angles = positions[:, None] * frequency[None, :]
    cos, sin = jnp.cos(angles), jnp.sin(angles)
    rest = HD - ROT
    zero = jnp.zeros((SEQ, rest), f32)
    keep = jnp.concatenate([cos, cos, jnp.ones((SEQ, rest), f32)], -1)
    ahead = jnp.concatenate([-sin, jnp.zeros_like(sin), zero], -1)
    behind = jnp.concatenate([jnp.zeros_like(sin), sin, zero], -1)
    one = jnp.stack([keep, ahead, behind])
    one = jnp.concatenate([one, one], -1).reshape(3, line, 2, -1, PAIR)
    return [one[:, :, t].reshape(3, SEQ // 2, PAIR) for t in range(2)]


def turned(v, tab_ref, sign):
    half_rot = ROT // 2
    return (
        v * tab_ref[0]
        + sign
        * (
            pltpu.roll(v, PAIR - half_rot, 1) * tab_ref[1]
            + pltpu.roll(v, half_rot, 1) * tab_ref[2]
        )
    )


def dot_nt(a, b):
    return lax.dot_general(a, b, (((1,), (1,)), ((), ())), preferred_element_type=f32)


def dot_nn(a, b):
    return lax.dot_general(a, b, (((1,), (0,)), ((), ())), preferred_element_type=f32)


def dot_tn(a, b):
    return lax.dot_general(a, b, (((0,), (0,)), ((), ())), preferred_element_type=f32)


def two_heads(a):
    lane = lax.broadcasted_iota(jnp.int32, a.shape, 1)
    zero = jnp.zeros_like(a)
    return jnp.concatenate([jnp.where(lane < HD, a, zero), jnp.where(lane < HD, zero, a)], 0)


def one_row_each(a):
    rows = a.shape[1] // 2
    dim = lax.broadcasted_iota(jnp.int32, (PAIR, rows), 0)
    return jnp.where(dim < HD, a[:, :rows], a[:, rows:]).T


def spans(part, z, span):
    return ((z + 1) * span, (z + part) * span)


def masked(a, span, fill):
    lo = a.shape[0] - span
    key = lax.broadcasted_iota(jnp.int32, (span, 2 * span), 0)
    query = lax.broadcasted_iota(jnp.int32, (span, 2 * span), 1)
    query = jnp.where(query >= span, query - span, query)
    tail = jnp.where(key <= query, a[lo:], fill)
    return jnp.concatenate([a[:lo], tail], 0) if lo else tail


def attend_kernel(part, span, q_ref, k0_ref, v0_ref, k1_ref, v1_ref, attn_ref, lse_ref):
    keys, values = (k0_ref, k1_ref), (v0_ref[0].T, v1_ref[0].T)
    for z in range(SEQ // 2 // span):
        rows = slice(z * span, (z + 1) * span)
        q = two_heads(q_ref[0, rows, :])
        scores = {}
        for t, count in enumerate(spans(part, z, span)):
            if count:
                scores[t] = dot_nt(keys[t][0, :count, :], q)
        scores[part] = masked(scores[part], span, -1e30)
        top = functools.reduce(
            jnp.maximum, [jnp.max(a, 0, keepdims=True) for a in scores.values()]
        )
        scores = {t: jnp.exp(a - top) for t, a in scores.items()}
        total = sum(jnp.sum(a, 0, keepdims=True) for a in scores.values())
        inverse = 1.0 / total
        out = sum(
            dot_nn(values[t][:, : a.shape[0]], (a * inverse).astype(bf16))
            for t, a in scores.items()
        )
        attn_ref[rows, :] = one_row_each(out).astype(bf16)
        lse_ref[0, z : z + 1, :] = top + jnp.log(total)


def head_spec(j):
    return pl.BlockSpec((1, SEQ // 2, PAIR), lambda p: (j, 0, p))


def attend(part, span, qkv):
    width = qkv[0].shape[2]
    pairs = width // PAIR
    blocks = SEQ // 2 // span
    half = SEQ // 2
    mine = pl.BlockSpec((half, PAIR), lambda p: (0, p))
    return pl.pallas_call(
        functools.partial(attend_kernel, part, span),
        grid=(pairs,),
        in_specs=[head_spec(0), head_spec(1), head_spec(2), head_spec(1), head_spec(2)],
        out_specs=[mine, pl.BlockSpec((1, blocks, 2 * span), lambda p: (p, 0, 0))],
        out_shape=[
            jax.ShapeDtypeStruct((half, width), bf16),
            jax.ShapeDtypeStruct((pairs, blocks, 2 * span), f32),
        ],
        compiler_params=pltpu.CompilerParams(vmem_limit_bytes=(56 if part else 30) << 20),
        cost_estimate=pl.CostEstimate(
            flops=pairs * SEQ * SEQ * PAIR * 4,
            transcendentals=pairs * SEQ * SEQ,
            bytes_accessed=10 * SEQ * width,
        ),
        name="attend",
    )(qkv[part], qkv[0], qkv[0], qkv[1], qkv[1])


def attend_back_kernel(
    part, span, q_ref, k0_ref, v0_ref, k1_ref, v1_ref, grad_ref, lse_ref, tab0_ref, tab1_ref, *refs
):
    scale = HD ** (-0.5)
    half = SEQ // 2
    if part == 0:
        gq_ref, *gkv_refs = refs
        sums = gkv_refs
        for ref in sums:
            ref[...] = jnp.zeros_like(ref)
    else:
        gq0_ref, *kept = refs[:5]
        out_ref, bias_ref, gq_ref, *sums = refs[5:]
        for ref, old in zip(sums, kept):
            ref[...] = old[...]
    keys, values = (k0_ref, k1_ref), (v0_ref, v1_ref)
    turned_keys = (k0_ref[0].T, k1_ref[0].T)
    for z in range(half // span):
        rows = slice(z * span, (z + 1) * span)
        q, g = two_heads(q_ref[0, rows, :]), two_heads(grad_ref[rows, :])
        lse = lse_ref[0, z : z + 1, :]
        probs, gprobs = {}, {}
        inner = 0.0
        for t, count in enumerate(spans(part, z, span)):
            if count:
                p = jnp.exp(dot_nt(keys[t][0, :count, :], q) - lse)
                probs[t] = masked(p, span, 0.0) if t == part else p
                gprobs[t] = dot_nt(values[t][0, :count, :], g)
                inner = inner + jnp.sum(probs[t] * gprobs[t], 0, keepdims=True)
        gq = 0.0
        for t, p in probs.items():
            count = p.shape[0]
            gs = (p * (gprobs[t] - inner)).astype(bf16)
            sums[2 * t][:count, :] += dot_nn(gs, q)
            sums[2 * t + 1][:count, :] += dot_nn(p.astype(bf16), g)
            gq = gq + dot_nn(turned_keys[t][:, :count], gs)
        gq_ref[rows, :] = one_row_each(gq) * scale
    if part == 1:
        pairs = pl.num_programs(0)
        pair = pl.program_id(0)
        for j in range(3):
            lanes = pl.ds(pl.multiple_of((j * pairs + pair) * PAIR, PAIR), PAIR)
            bias = 0.0
            for t, tab_ref in enumerate((tab0_ref, tab1_ref)):
                g = sums[2 * t + j - 1][...] if j else (gq_ref if t else gq0_ref)[...]
                if j < 2:
                    g = turned(g, tab_ref, -1.0)
                g = g.astype(bf16)
                out_ref[t * half : (t + 1) * half, lanes] = g
                bias = bias + jnp.sum(g.astype(f32).reshape(half // 8, 8, PAIR), 0)
            bias_ref[:, lanes] = bias


def attend_back(part, span, qkv, grad, lse, tables, kept=()):
    width = grad.shape[1]
    pairs = width // PAIR
    blocks = SEQ // 2 // span
    half = SEQ // 2
    mine = pl.BlockSpec((half, PAIR), lambda p: (0, p))
    table = pl.BlockSpec((3, half, PAIR), lambda p: (0, 0, 0))
    partial_shapes = [jax.ShapeDtypeStruct((half, width), f32)] * 5
    if part == 0:
        out_specs, out_shape, scratch = [mine] * 5, partial_shapes, []
    else:
        out_specs = [
            pl.BlockSpec((SEQ, 3 * width), lambda p: (0, 0)),
            pl.BlockSpec((8, 3 * width), lambda p: (0, 0)),
        ]
        out_shape = [
            jax.ShapeDtypeStruct((SEQ, 3 * width), bf16),
            jax.ShapeDtypeStruct((8, 3 * width), f32),
        ]
        scratch = [pltpu.VMEM((half, PAIR), f32)] * 5
    return pl.pallas_call(
        functools.partial(attend_back_kernel, part, span),
        grid=(pairs,),
        in_specs=[head_spec(0), head_spec(1), head_spec(2), head_spec(1), head_spec(2)]
        + [mine, pl.BlockSpec((1, blocks, 2 * span), lambda p: (p, 0, 0)), table, table]
        + [mine] * len(kept),
        out_specs=out_specs,
        out_shape=out_shape,
        scratch_shapes=scratch,
        compiler_params=pltpu.CompilerParams(vmem_limit_bytes=(56 if part else 30) << 20),
        cost_estimate=pl.CostEstimate(
            flops=pairs * SEQ * SEQ * PAIR * 10,
            transcendentals=pairs * SEQ * SEQ,
            bytes_accessed=20 * SEQ * width,
        ),
        name="attend_back",
    )(qkv[part], qkv[0], qkv[0], qkv[1], qkv[1], grad, lse, *tables, *kept)


def call(kernel, name, grid, in_specs, out_specs, out_shape, scalars, args, flops=0, scratch=(), vmem=30):
    moved = sum(a.size * a.dtype.itemsize for a in args)
    moved += sum(o.size * jnp.dtype(o.dtype).itemsize for o in out_shape)
    return pl.pallas_call(
        kernel,
        grid_spec=pltpu.PrefetchScalarGridSpec(
            num_scalar_prefetch=1,
            grid=grid,
            in_specs=in_specs,
            out_specs=out_specs,
            scratch_shapes=scratch,
        ),
        out_shape=out_shape,
        compiler_params=pltpu.CompilerParams(vmem_limit_bytes=vmem << 20),
        cost_estimate=pl.CostEstimate(flops=flops, transcendentals=0, bytes_accessed=moved),
        name=name,
    )(scalars, *args)


def whole_spec(shape):
    zeros = (0,) * len(shape)
    return pl.BlockSpec(shape, lambda i, s: zeros, pipeline_mode=pl.Buffered(1))


def shard_spec(w):
    rest = (0,) * (w.ndim - 1)
    return pl.BlockSpec((1,) + w.shape[1:], lambda k, s: (k,) + rest)


def all_spec(rows, cols):
    return pl.BlockSpec((rows, cols), lambda k, s: (0, 0), pipeline_mode=pl.Buffered(1))


def over_rows(rows, step, body):
    @pl.loop(0, rows // step)
    def _(i):
        body(pl.ds(pl.multiple_of(i * step, step), step))


def row_spec(rows, cols):
    return pl.BlockSpec((rows, cols), lambda i, s: (i, 0))


def shape_of(shape, dtype):
    return jax.ShapeDtypeStruct(shape, dtype)


def lanes_of(scalar_ref, h, p, feats):
    block = 2 * p + jnp.bitwise_xor(scalar_ref[0], h)
    return pl.ds(pl.multiple_of(block * feats, feats), feats)


def shard_lanes(scalar_ref, k, feats, first=0):
    block = jnp.bitwise_xor(scalar_ref[1], k)
    return pl.ds(pl.multiple_of(first + block * feats, feats), feats)


def moments(x):
    mean = jnp.sum(x, -1, keepdims=True) / D
    x = x - mean
    return mean, lax.rsqrt(jnp.sum(x * x, -1, keepdims=True) / D + epsilon)


def norm_kernel(feats, s_ref, x_ref, vec_ref, own_ref, other_ref, stat_ref, copy_ref):
    mean, inv = moments(x_ref[...].astype(f32))
    copy_ref[...] = x_ref[...]
    for h, out_ref in enumerate((own_ref, other_ref)):
        for p in range(D // (2 * feats)):
            at = lanes_of(s_ref, h, p, feats)
            u = (x_ref[:, at].astype(f32) - mean) * inv
            out_ref[:, p * feats : (p + 1) * feats] = (
                u * vec_ref[0:1, at] + vec_ref[1:2, at]
            ).astype(bf16)
    lane = lax.broadcasted_iota(jnp.int32, stat_ref.shape, 1)
    stat_ref[...] = jnp.where(lane < PAIR // 2, mean, inv)


def norm(scalars, part, span, x, vectors, feats):
    half = D // 2
    rows = SEQ // 2
    return call(
        functools.partial(norm_kernel, feats),
        "norm",
        (rows // span,),
        [pl.BlockSpec((span, D), lambda z, s: (2 * z + part, 0)), whole_spec((2, D))],
        [row_spec(span, half), row_spec(span, half), row_spec(span, PAIR), row_spec(span, D)],
        [shape_of((rows, half), bf16)] * 2
        + [shape_of((rows, PAIR), f32), shape_of((rows, D), bf16)],
        scalars,
        (x, vectors),
    )


def joined_kernel(
    s_ref, own_ref, other_ref, bias_ref, tab_ref, w0_ref, w1_ref, out_ref, sum_ref
):
    _, many, feats, width = w0_ref.shape
    k, last_k = pl.program_id(0), pl.num_programs(0) - 1
    at = shard_lanes(s_ref, k, feats)
    rows = own_ref.shape[0]

    @pl.when(k == 0)
    def _():
        for j in range(many):
            sum_ref[j] = jnp.broadcast_to(bias_ref[j], (rows, width))

    def step(here):
        x0, x1 = own_ref[here, at], other_ref[here, at]
        for j in range(many):
            sum_ref[j, here, :] += dot_nn(x0, w0_ref[0, j]) + dot_nn(x1, w1_ref[0, j])

    over_rows(rows, SPAN, step)

    @pl.when(k == last_k)
    def _():
        def rotate(here):
            tab = tab_ref[:, here, :]
            for j in range(2):
                scale = 1.0 if j else HD ** (-0.5)
                for p in range(width // PAIR):
                    lanes = slice(p * PAIR, (p + 1) * PAIR)
                    out_ref[j, here, lanes] = (
                        turned(sum_ref[j, here, lanes], tab, 1.0) * scale
                    ).astype(bf16)
            out_ref[2, here, :] = sum_ref[2, here, :].astype(bf16)

        over_rows(rows, 64, rotate)


def joined_heads(scalars, normed, weights, bias, table):
    chips, many, _, width = weights[0].shape
    rows = normed[0].shape[0]
    return call(
        joined_kernel,
        "joined",
        (chips,),
        [all_spec(rows, D // 2)] * 2
        + [whole_spec((3, 1, width)), whole_spec((3, rows, PAIR))]
        + [shard_spec(w) for w in weights],
        [pl.BlockSpec((3, rows, width), lambda k, s: (0, 0, 0))],
        [shape_of((3, rows, width), bf16)],
        scalars,
        (*normed, bias, table, *weights),
        flops=2 * rows * D * 3 * width,
        scratch=[pltpu.VMEM((many, rows, width), f32)],
    )[0]


def gate_up_kernel(
    s_ref, own_ref, other_ref, attn_ref, w0_ref, w1_ref, gate_ref, up_ref, acts_ref
):
    width = attn_ref.shape[1]
    feats = w0_ref.shape[2]
    k, last_k = pl.program_id(0), pl.num_programs(0) - 1
    at = shard_lanes(s_ref, k, feats)
    rows = own_ref.shape[0]

    @pl.when(k == 0)
    def _():
        gate_ref[...] = jnp.zeros_like(gate_ref)
        up_ref[...] = jnp.zeros_like(up_ref)
        acts_ref[:, :width] = attn_ref[...]

    def step(here):
        x0, x1 = own_ref[here, at], other_ref[here, at]
        for j, out_ref in enumerate((gate_ref, up_ref)):
            out_ref[here, :] += dot_nn(x0, w0_ref[0, j]) + dot_nn(x1, w1_ref[0, j])

    over_rows(rows, SPAN, step)

    @pl.when(k == last_k)
    def _():
        def join(here):
            gate = gate_ref[here, :]
            acts_ref[here, width:] = (gate * jax.nn.sigmoid(gate) * up_ref[here, :]).astype(bf16)

        over_rows(rows, 64, join)


def gate_up(scalars, normed, attn, weights):
    chips, _, _, hid = weights[0].shape
    rows, width = attn.shape
    return call(
        gate_up_kernel,
        "gate_up",
        (chips,),
        [all_spec(rows, D // 2)] * 2
        + [all_spec(rows, width)]
        + [shard_spec(w) for w in weights],
        [all_spec(rows, hid), all_spec(rows, hid), all_spec(rows, width + hid)],
        [shape_of((rows, hid), f32)] * 2 + [shape_of((rows, width + hid), bf16)],
        scalars,
        (*normed, attn, *weights),
        flops=4 * rows * D * hid,
    )


def branch_kernel(s_ref, acts_ref, w0_ref, w1_ref, out_ref):
    feats = w0_ref.shape[2]
    p = pl.program_id(0)
    rows = acts_ref.shape[0]

    def step(here):
        acts = acts_ref[here, :]
        for h, w_ref in enumerate((w0_ref, w1_ref)):
            at = pl.ds(pl.multiple_of(h * D // 2 + p * feats, feats), feats)
            out_ref[here, at] = dot_nn(acts, w_ref[0]).astype(bf16)

    over_rows(rows, SPAN, step)


def branch_sums(scalars, acts, weights):
    chips = weights[0].shape[0]
    rows, deep = acts.shape
    return call(
        branch_kernel,
        "branch",
        (chips,),
        [all_spec(rows, deep)] + [shard_spec(w) for w in weights],
        [all_spec(rows, D)],
        [shape_of((rows, D), bf16)],
        scalars,
        (acts, *weights),
        flops=2 * rows * deep * D,
    )[0]


def finish_kernel(
    feats, part, s_ref, branch_ref, x_ref, teach_ref, cot_ref, old_ref,
    result_ref, seed_ref, low_ref, loss_ref,
):
    rows = x_ref.shape[0]
    first = (2 * s_ref[2] + part) * rows
    valid = (first + lax.broadcasted_iota(jnp.int32, (rows, 1), 0) < s_ref[3]).astype(f32)
    loss = jnp.zeros((8, PAIR), f32)
    chips = D // (2 * feats)
    for h in range(2):
        for k in range(chips):
            at = lanes_of(s_ref, h, k, feats)
            here = slice((h * chips + k) * feats, (h * chips + k + 1) * feats)
            y = x_ref[:, at].astype(f32) + valid * branch_ref[:, here].astype(f32)
            mismatch = y - teach_ref[:, at].astype(f32)
            square = jnp.sum((valid * mismatch * mismatch).reshape(rows // 8, 8, feats), 0)
            for q in range(feats // PAIR):
                loss = loss + square[:, q * PAIR : (q + 1) * PAIR]
            seed = valid * (cot_ref[:, at].astype(f32) + mismatch)
            result_ref[:, at] = y.astype(bf16)
            seed_ref[:, at] = seed
            low_ref[:, here] = seed.astype(bf16)
    loss_ref[...] = loss


def part_spec(rows, cols, part):
    return pl.BlockSpec((rows, cols), lambda i, s: (part, 0))


def aliased(kernel, name, in_specs, out_specs, out_shape, scalars, args, aliases):
    moved = sum(o.size * jnp.dtype(o.dtype).itemsize for o in out_shape)
    return pl.pallas_call(
        kernel,
        grid_spec=pltpu.PrefetchScalarGridSpec(
            num_scalar_prefetch=1, grid=(1,), in_specs=in_specs, out_specs=out_specs
        ),
        out_shape=out_shape,
        input_output_aliases=aliases,
        compiler_params=pltpu.CompilerParams(vmem_limit_bytes=24 << 20),
        cost_estimate=pl.CostEstimate(flops=0, transcendentals=0, bytes_accessed=3 * moved),
        name=name,
    )(scalars, *args)


def finish(scalars, part, branch, x, teacher, out_grad, old, feats):
    rows = branch.shape[0]
    mine = part_spec(rows, D, part)
    one = part_spec(rows, D, 0)
    aliases = {}
    if old is None:
        old = jnp.zeros((8, PAIR), bf16)
        old_spec = part_spec(8, PAIR, 0)
    else:
        old_spec = pl.BlockSpec(memory_space=pl.ANY)
        aliases = {5: 0}
    return aliased(
        functools.partial(finish_kernel, feats, part),
        "finish",
        [one, mine, mine, mine, old_spec],
        [mine, one, one, part_spec(8, PAIR, 0)],
        [
            shape_of((2 * rows, D), bf16),
            shape_of((rows, D), f32),
            shape_of((rows, D), bf16),
            shape_of((8, PAIR), f32),
        ],
        scalars,
        (branch, x, teacher, out_grad, old),
        aliases,
    )


def grad_acts_kernel(
    s_ref, seed_ref, gate_ref, up_ref, w0_ref, w1_ref, attn_ref, gu_ref, sum_ref
):
    hid = gate_ref.shape[1]
    width = attn_ref.shape[1]
    feats = w0_ref.shape[2]
    p, last_p = pl.program_id(0), pl.num_programs(0) - 1
    rows = seed_ref.shape[0]

    @pl.when(p == 0)
    def _():
        sum_ref[...] = jnp.zeros_like(sum_ref)

    def step(here):
        total = sum_ref[here, :]
        for h, w_ref in enumerate((w0_ref, w1_ref)):
            at = pl.ds(pl.multiple_of(h * D // 2 + p * feats, feats), feats)
            total = total + dot_nt(seed_ref[here, at], w_ref[0])
        sum_ref[here, :] = total

    over_rows(rows, SPAN, step)

    @pl.when(p == last_p)
    def _():
        def split(here):
            attn_ref[here, :] = sum_ref[here, :width].astype(bf16)
            grad = sum_ref[here, width:]
            gate, up = gate_ref[here, :], up_ref[here, :]
            sigmoid = jax.nn.sigmoid(gate)
            gu_ref[here, :hid] = (
                grad * up * sigmoid * (1.0 + gate * (1.0 - sigmoid))
            ).astype(bf16)
            gu_ref[here, hid:] = (grad * gate * sigmoid).astype(bf16)

        over_rows(rows, 64, split)


def grad_acts(scalars, seed, weights, gate, up):
    chips, deep, _ = weights[0].shape
    rows, hid = gate.shape
    width = deep - hid
    return call(
        grad_acts_kernel,
        "grad_acts",
        (chips,),
        [all_spec(rows, D), all_spec(rows, hid), all_spec(rows, hid)]
        + [shard_spec(w) for w in weights],
        [all_spec(rows, width), all_spec(rows, 2 * hid)],
        [shape_of((rows, width), bf16), shape_of((rows, 2 * hid), bf16)],
        scalars,
        (seed, gate, up, *weights),
        flops=2 * rows * D * deep,
        scratch=[pltpu.VMEM((rows, deep), f32)],
    )


def grad_normed_kernel(s_ref, qkv_ref, gu_ref, x_ref, stat_ref, *refs):
    w_refs, (out_ref, gain_ref, shift_ref) = refs[:4], refs[4:]
    feats = w_refs[0].shape[2]
    k = pl.program_id(0)
    rows = x_ref.shape[0]
    at = [shard_lanes(s_ref, k, feats, h * D // 2) for h in range(2)]
    for h in range(2):
        gain_ref[:, at[h]] = jnp.zeros((8, feats), f32)
        shift_ref[:, at[h]] = jnp.zeros((8, feats), f32)

    def step(here):
        mean, inv = stat_ref[here, 0:1], stat_ref[here, PAIR // 2 : PAIR // 2 + 1]
        for h in range(2):
            g = 0.0
            for a_ref, w_ref in ((qkv_ref, w_refs[h]), (gu_ref, w_refs[2 + h])):
                _, many, _, wide = w_ref.shape
                for j in range(many):
                    g = g + dot_nt(a_ref[here, j * wide : (j + 1) * wide], w_ref[0, j])
            out_ref[here, at[h]] = g.astype(bf16)
            lanes = lanes_of(s_ref, h, jnp.bitwise_xor(s_ref[1], k), feats)
            u = (x_ref[here, lanes].astype(f32) - mean) * inv
            gain_ref[:, at[h]] += jnp.sum((g * u).reshape(-1, 8, feats), 0)
            shift_ref[:, at[h]] += jnp.sum(g.reshape(-1, 8, feats), 0)

    over_rows(rows, SPAN, step)


def grad_normed(scalars, part, grad_qkv, grad_gu, w_qkv, w_gu, x, stats):
    chips, _, _, width = w_qkv[0].shape
    hid = w_gu[0].shape[3]
    rows = x.shape[0]
    weights = (*w_qkv, *w_gu)
    return call(
        grad_normed_kernel,
        "grad_normed",
        (chips,),
        [
            pl.BlockSpec((rows, 3 * width), lambda k, s: (part, 0)),
            all_spec(rows, 2 * hid),
            all_spec(rows, D),
            all_spec(rows, PAIR),
        ]
        + [shard_spec(w) for w in weights],
        [all_spec(rows, D), all_spec(8, D), all_spec(8, D)],
        [shape_of((rows, D), bf16), shape_of((8, D), f32), shape_of((8, D), f32)],
        scalars,
        (grad_qkv, grad_gu, x, stats, *weights),
        flops=2 * rows * D * (3 * width + 2 * hid),
        vmem=56 if part else 30,
    )


def last_kernel(feats, s_ref, sum_ref, x_ref, vec_ref, seed_ref, old_ref, out_ref):
    mean, inv = moments(x_ref[...].astype(f32))
    chips = D // (2 * feats)

    def units(h, k):
        here = slice((h * chips + k) * feats, (h * chips + k + 1) * feats)
        at = lanes_of(s_ref, h, k, feats)
        g = sum_ref[:, here].astype(f32) * vec_ref[0:1, at]
        return g, (x_ref[:, at].astype(f32) - mean) * inv, at

    m1 = m2 = 0.0
    for h in range(2):
        for k in range(chips):
            g, u, _ = units(h, k)
            m1 = m1 + jnp.sum(g, -1, keepdims=True)
            m2 = m2 + jnp.sum(g * u, -1, keepdims=True)
    m1, m2 = m1 / D, m2 / D
    for h in range(2):
        for k in range(chips):
            g, u, at = units(h, k)
            out_ref[:, at] = (seed_ref[:, at] + inv * (g - m1 - u * m2)).astype(bf16)


def last(scalars, part, total, x, vectors, seed, old, feats):
    rows = total.shape[0]
    mine = part_spec(rows, D, part)
    one = part_spec(rows, D, 0)
    aliases = {}
    if old is None:
        old = jnp.zeros((8, PAIR), bf16)
        old_spec = part_spec(8, PAIR, 0)
    else:
        old_spec = pl.BlockSpec(memory_space=pl.ANY)
        aliases = {5: 0}
    return aliased(
        functools.partial(last_kernel, feats),
        "last",
        [one, mine, part_spec(2, D, 0), one, old_spec],
        [mine],
        [shape_of((2 * rows, D), bf16)],
        scalars,
        (total, x, vectors, seed, old),
        aliases,
    )[0]


def per_device(
    chips,
    line,
    layer_input,
    teacher,
    out_grad,
    lengths,
    norm_gain,
    norm_bias,
    qkv_weight,
    qkv_bias,
    out_weight,
    gate_up_weight,
    down_weight,
):
    core = lax.axis_index("core")
    chip = lax.axis_index("chip")
    place = lax.axis_index("tp")
    scalars = jnp.stack([core, chip, place, lengths[0]]).astype(jnp.int32)
    feats = D // (2 * chips)
    width = qkv_weight.shape[2]
    hid = down_weight.shape[0]
    n = norm_gain.shape[0]
    cat = jnp.concatenate

    def to_chip(a, k):
        return lax.ppermute(a, "chip", [(c, c ^ k) for c in range(chips)])

    def near_shards(w):
        if chips != 4:
            every = lax.all_gather(w, "chip", axis=0, tiled=False)
            return [
                lax.dynamic_index_in_dim(every, chip ^ k, 0, keepdims=False)
                for k in range(1, chips)
            ]
        return [to_chip(w, 1), to_chip(w, 2)]

    def far_shard(near):
        if chips != 4:
            return []
        cut = feats // 2
        return [cat([to_chip(near[0][:, :cut], 2), to_chip(near[1][:, cut:], 1)], 1)]

    def both_cores(own):
        return [own, swap_core(own)]

    small = cat([norm_gain, norm_bias, qkv_bias.astype(f32).reshape(-1)])
    small = gather_axis(gather_axis(small, "core", 2), "chip", chips)
    small = small.reshape(2 * chips, -1)
    bias = small[:, 2 * n :].reshape(2 * chips, 3, -1)
    bias = bias.transpose(1, 0, 2).reshape(3, 1, width)
    vectors = gather_axis(small[:, : 2 * n], "tp", line)
    vectors = vectors.reshape(line, 2 * chips, 2, n).transpose(2, 1, 0, 3).reshape(2, D)

    rows = layer_input.shape[0]
    span = rows // 2
    tables = rotary_tables(line)

    def along_line(a):
        return lax.all_gather(a, "tp", axis=0, tiled=True)

    def summed_line(a):
        return lax.psum_scatter(a, "tp", scatter_dimension=0, tiled=True)

    slot = along_line(layer_input)
    w_od = lax.all_gather(cat([out_weight, down_weight], 0), "chip", axis=0, tiled=False)
    shard = after(gate_up_weight, small)
    near = near_shards(shard)
    slot = after(slot, *near)
    qkv_shard = after(qkv_weight, vectors, *tables, *near)
    w_gu = both_cores(jnp.stack([shard, *near, *far_shard(near)]))
    near = near_shards(qkv_shard)
    w_qkv = both_cores(jnp.stack([qkv_shard, *near, *far_shard(near)]))
    normed, stats, x, qkv = [None] * 2, [None] * 2, [None] * 2, [None] * 2
    for t in range(2):
        *normed[t], stats[t], x[t] = norm(scalars, t, span, slot, vectors, feats)
    for t in range(2):
        qkv[t] = joined_heads(scalars, normed[t], w_qkv, bias, tables[t])
    gate, up, acts = [None] * 2, [None] * 2, [None] * 2
    attn, lse, branch = [None] * 2, [None] * 2, [None] * 2
    attn[0], lse[0] = attend(0, span, qkv)
    w_od = both_cores(after(w_od, attn[0]))
    gate[0], up[0], acts[0] = gate_up(scalars, normed[0], attn[0], w_gu)
    branch[0] = branch_sums(scalars, acts[0], w_od)
    qkv[1] = after(qkv[1], branch[0])
    attn[1], lse[1] = attend(1, span, qkv)
    gate[1], up[1], acts[1] = gate_up(scalars, normed[1], attn[1], w_gu)
    branch[1] = branch_sums(scalars, acts[1], w_od)
    seeds, seed_all, losses = [None] * 2, [None] * 2, [None] * 2
    result = None
    for t in range(2):
        total = summed_line(branch[t])
        result, seeds[t], low, loss = finish(
            scalars, t, total, layer_input, teacher, out_grad, result, feats
        )
        losses[t] = jnp.sum(loss)
        seed_all[t] = along_line(low)

    half = D // 2

    def with_other(mine, theirs):
        return (mine + theirs.astype(f32)).astype(bf16)

    def scattered(a, axis):
        return lax.psum_scatter(a, "chip", scatter_dimension=axis, tiled=True).astype(f32)

    def rows_of(a, k):
        return lax.dynamic_slice_in_dim(a, (chip ^ k) * feats, feats, 0)

    def sent_rows(a, some):
        return [to_chip(rows_of(a, k), k) for k in some]

    acts_all = cat(acts, 0)
    normed_all = [cat([normed[0][h], normed[1][h]], 0) for h in range(2)]
    grad_attn, grad_gu = [None] * 2, [None] * 2
    grad_attn[0], grad_gu[0] = grad_acts(scalars, seed_all[0], w_od, gate[0], up[0])
    kept = attend_back(0, span, qkv, grad_attn[0], lse[0], tables)

    seed_all[1] = after(seed_all[1], kept[0], acts_all, *normed_all)
    seeds_all = cat(seed_all, 0)
    od_sent = dot_tn(acts_all, seeds_all[:, half:]).astype(bf16)
    od_theirs = swap_core(od_sent)
    seed_all[1] = after(seed_all[1], od_sent)
    grad_attn[1], grad_gu[1] = grad_acts(scalars, seed_all[1], w_od, gate[1], up[1])
    od_sum = dot_tn(acts_all, after(seeds_all, grad_gu[1])[:, :half])
    od_sum = with_other(od_sum, od_theirs)
    od_grad = scattered(od_sum, 1)
    gu_all = cat([grad_gu[0], after(grad_gu[1], od_sum)], 0)
    gu_sent = dot_tn(normed_all[1], gu_all).astype(bf16)
    gu_theirs = swap_core(gu_sent)
    grad_qkv, grad_bias = attend_back(
        1, span, qkv, after(grad_attn[1], gu_sent), lse[1], tables, kept
    )
    gu_sum = with_other(dot_tn(normed_all[0], after(gu_all, grad_qkv)), gu_theirs)
    grads, gains, shifts, sums = [None] * 2, [None] * 2, [None] * 2, [None] * 2

    def back(t, *hold):
        grads[t], gain, shift = grad_normed(
            scalars, t, after(grad_qkv, *hold), grad_gu[t], w_qkv, w_gu, x[t], stats[t]
        )
        gains[t], shifts[t] = jnp.sum(gain, 0), jnp.sum(shift, 0)
        sums[t] = summed_line(grads[t])

    qkv_held = after(grad_qkv, gu_sum)
    qkv_sent = dot_tn(normed_all[1], qkv_held).astype(bf16)
    qkv_theirs = swap_core(qkv_sent)
    gu_got = sent_rows(gu_sum, (1, 2))
    back(0, qkv_sent)
    qkv_back = after(grad_qkv, grads[0], *gu_got)
    gu_got += sent_rows(after(gu_sum, qkv_back), range(3, chips))
    back(1, qkv_back)
    qkv_held = after(qkv_held, grads[1], *gu_got)
    qkv_sum = with_other(dot_tn(normed_all[0], qkv_held), qkv_theirs)
    qkv_got = sent_rows(qkv_sum, range(1, chips))
    gu_grad = rows_of(gu_sum, 0).astype(f32) + sum(g.astype(f32) for g in gu_got)
    qkv_grad = rows_of(qkv_sum, 0).astype(f32) + sum(g.astype(f32) for g in qkv_got)
    input_grad = None
    for t in range(2):
        input_grad = last(
            scalars, t, sums[t], layer_input, vectors, seeds[t], input_grad, feats
        )
    gains = [(gains[0] + gains[1])[h * half : (h + 1) * half] for h in range(2)]
    shifts = [(shifts[0] + shifts[1])[h * half : (h + 1) * half] for h in range(2)]

    count = jnp.clip(lengths[0] - place * rows, 0, rows)
    scalar_sums = jnp.stack([losses[0] + losses[1], count.astype(f32)])
    scalar_sums = jnp.broadcast_to(scalar_sums, (chips, line, 2))
    heads = jnp.sum(grad_bias, 0).reshape(3, chips, 2, -1).transpose(2, 1, 0, 3)
    heads = [jnp.where(core == h, heads[0], heads[1]) for h in range(2)]
    small_sums = []
    for h in range(2):
        vector = jnp.stack([gains[h], shifts[h]]).reshape(2, chips, line, n)
        vector = cat([vector.transpose(1, 2, 0, 3).reshape(chips, line, 2 * n), scalar_sums], -1)
        small_sums.append(cat([vector.reshape(chips, -1), heads[h].reshape(chips, -1)], -1))
    small_sums = [after(v, qkv_got[0]) for v in small_sums]
    total = direct_sum(small_sums[0] + swap_core(small_sums[1]), "chip", chips)
    cut = line * (2 * n + 2)
    qkv_b_grad = total[cut:].reshape(3, -1)
    total = after(total[:cut], input_grad).reshape(line, -1)
    total = direct_sum(total, "tp", line)
    gain_grad, bias_grad = total[:n], total[n : 2 * n]
    loss_value = total[2 * n] / (total[2 * n + 1] * D)
    return (
        result,
        loss_value,
        input_grad,
        gain_grad,
        bias_grad,
        jnp.stack([qkv_grad[:, j * width : (j + 1) * width] for j in range(3)]),
        qkv_b_grad,
        od_grad[:width],
        jnp.stack([gu_grad[:, j * hid : (j + 1) * hid] for j in range(2)]),
        od_grad[width:],
    )


def solution(mesh):
    chips, line = mesh.shape["fsdp"] // 2, mesh.shape["tp"]
    fine = Mesh(mesh.devices.reshape(chips, 2, line), ("chip", "core", "tp"))
    fsdp = ("chip", "core")
    tokens = P(fsdp + ("tp",), None)
    vector = P(fsdp + ("tp",))
    return jax.shard_map(
        functools.partial(per_device, chips, line),
        mesh=fine,
        in_specs=(
            tokens,
            tokens,
            tokens,
            P(fsdp),
            vector,
            vector,
            P(None, fsdp, "tp"),
            P(None, ("tp",) + fsdp),
            P("tp", fsdp),
            P(None, fsdp, "tp"),
            P("tp", fsdp),
        ),
        out_specs=(
            tokens,
            P(),
            tokens,
            vector,
            vector,
            P(None, fsdp, "tp"),
            P(None, ("tp",) + fsdp),
            P("tp", fsdp),
            P(None, fsdp, "tp"),
            P("tp", fsdp),
        ),
        check_vma=False,
    )
```
